256 devices in a mesh: row: 32 (over z, x_lo, core), head: 8 (over y, x_hi).
Axes of the slice: x: 4 (x_hi: 2, x_lo: 2; x = x_hi * 2 + x_lo), y: 4, z: 8, core: 2. Of those that a mesh axis runs over, the one named last changes fastest.
Arguments:
- sequence_matrix: float32 [64, 512, 256], P('row', 'head'), may hold values from -6 to 6
- pair_representation: float32 [512, 512, 128], P('row', 'head'), may hold values from -6 to 6
- alignment_row_mask: int32 [64], P('row'), may hold values 0 or 1
- residue_mask: int32 [512], replicated, may hold values 0 or 1
- attention_scale_vector: float32 [256], replicated, may hold values from 0.1 to 1.9
- asking_factor_matrix: float32 [256, 256], replicated, may hold values from -0.375 to 0.375
- lookup_factor_matrix: float32 [256, 256], replicated, may hold values from -0.375 to 0.375
- content_factor_matrix: float32 [256, 256], replicated, may hold values from -0.375 to 0.375
- sigmoid_factor_matrix: float32 [256, 256], replicated, may hold values from -0.375 to 0.375
- final_factor_matrix: float32 [256, 256], replicated, may hold values from -0.375 to 0.375
- pair_norm_gain: float32 [128], replicated, may hold values from 0.1 to 1.9
- bias_weight: float32 [128, 8], replicated, may hold values from -20 to 20
- tensor_scale_vector: float32 [256], replicated, may hold values from 0.1 to 1.9
- first_factor_matrix: float32 [256, 32], replicated, may hold values from -0.375 to 0.375
- second_factor_matrix: float32 [256, 32], replicated, may hold values from -0.375 to 0.375
- outer_weight: float32 [1024, 128], replicated, may hold values from -1 to 1
Outputs:
- msa_out: float32 [64, 512, 256], P('row', 'head')
- pair_out: float32 [512, 512, 128], P('row', 'head')
The draws below stay inside these ranges and needn't reach their ends.
All inputs are finite; a program needn't handle non-finite values. No bound on the sum of `alignment_row_mask` on one device may be relied on, other than what follows from the above.
Results may differ from the reference program's by a relative error of at most 0.0003.
Values sent between devices are 32-bit elements; how exact they have to be, the bound alone decides.
No kernel may reach another device: no remote copies, remote signals or barrier semaphores. Data moves between devices by JAX's collectives and lax.ppermute only.
A program may use at most 64 MiB of HBM per device.

```python
import math
import jax
import jax.numpy as jnp
from jax import lax

FEATURE_DEPTH = 256
C_Z = 128
ATTENTION_GROUPS = 8
TENSOR_FACTOR = 32
CROP_LENGTH = 512
SEQUENCE_TOTAL = 64
N_ROW = 32


def draw_bias_weight(key, part):
    normal_draw = jnp.clip(jax.random.normal(key, (C_Z, ATTENTION_GROUPS), jnp.float32), -4.0, 4.0)
    return normal_draw / math.sqrt(C_Z)


def touch_ends(drawn, own_key, least, high):
    spot = [jax.random.randint(jax.random.fold_in(own_key, axis), (), 0, length) for axis, length in enumerate(drawn.shape)]
    longest = drawn.shape.index(max(drawn.shape))
    beside = spot[:longest] + [(spot[longest] + 1) % drawn.shape[longest]] + spot[longest + 1:]
    return drawn.at[tuple(spot)].set(least).at[tuple(beside)].set(high)


def levels(stream_key, shape, pieces, smallest, top_value):
    def one(axis_at, blocks):
        steps = jax.random.uniform(jax.random.fold_in(jax.random.fold_in(stream_key, 6), axis_at), (blocks,), jnp.float32, smallest / len(pieces), top_value / len(pieces))
        return jnp.repeat(jnp.exp(steps), shape[axis_at] // blocks).reshape((-1,) + (1,) * (len(shape) - axis_at - 1))

    gain = one(*pieces[0])
    for cut in pieces[1:]:
        gain = gain * one(*cut)
    return gain


def noise(stream_key, dims, scale, bound, shards=(), held_as=jnp.bfloat16):
    factor_of = levels(stream_key, dims, shards, -0.22, 0.18) if shards else 1.0
    entries = jax.random.normal(stream_key, dims, jnp.float32) * scale * factor_of
    return jnp.minimum(jnp.maximum(entries, -bound), bound).astype(held_as)


def setup_inputs(seed: int = 0) -> dict:
    seeds = jax.random.split(jax.random.key(seed), 17)
    sequence_matrix = noise(seeds[0], (SEQUENCE_TOTAL, CROP_LENGTH, FEATURE_DEPTH), 1.0, 6.0, ((0, 32), (1, 8)), jnp.float32)
    pair_representation = noise(seeds[1], (CROP_LENGTH, CROP_LENGTH, C_Z), 1.0, 6.0, ((0, 32), (1, 8)), jnp.float32)
    alignment_row_mask = touch_ends((jax.random.randint(seeds[2], (SEQUENCE_TOTAL,), 0, 4) < 3).astype(jnp.int32), jax.random.fold_in(seeds[2], 1), 0, 1)
    residue_mask = touch_ends((jax.random.randint(seeds[3], (CROP_LENGTH,), 0, 8) < 7).astype(jnp.int32), jax.random.fold_in(seeds[3], 1), 0, 1)
    attention_scale_vector = jnp.clip(1.0 + 0.18 * jax.random.normal(seeds[4], (FEATURE_DEPTH,), jnp.float32), 0.1, 1.9)
    asking_factor_matrix = noise(seeds[5], (FEATURE_DEPTH, FEATURE_DEPTH), FEATURE_DEPTH ** -0.5, 0.375, (), jnp.float32)
    lookup_factor_matrix = noise(seeds[6], (FEATURE_DEPTH, FEATURE_DEPTH), FEATURE_DEPTH ** -0.5, 0.375, (), jnp.float32)
    content_factor_matrix = noise(seeds[7], (FEATURE_DEPTH, FEATURE_DEPTH), FEATURE_DEPTH ** -0.5, 0.375, (), jnp.float32)
    sigmoid_factor_matrix = noise(seeds[8], (FEATURE_DEPTH, FEATURE_DEPTH), FEATURE_DEPTH ** -0.5, 0.375, (), jnp.float32)
    final_factor_matrix = noise(seeds[9], (FEATURE_DEPTH, FEATURE_DEPTH), FEATURE_DEPTH ** -0.5, 0.375, (), jnp.float32)
    pair_norm_gain = jnp.clip(1.0 + 0.18 * jax.random.normal(seeds[10], (C_Z,), jnp.float32), 0.1, 1.9)
    bias_weight = draw_bias_weight(jax.random.fold_in(seeds[16], 71), 0)
    tensor_scale_vector = jnp.clip(1.0 + 0.18 * jax.random.normal(seeds[12], (FEATURE_DEPTH,), jnp.float32), 0.1, 1.9)
    first_factor_matrix = noise(seeds[13], (FEATURE_DEPTH, TENSOR_FACTOR), FEATURE_DEPTH ** -0.5, 0.375, (), jnp.float32)
    second_factor_matrix = noise(seeds[14], (FEATURE_DEPTH, TENSOR_FACTOR), FEATURE_DEPTH ** -0.5, 0.375, (), jnp.float32)
    outer_weight = noise(seeds[15], (TENSOR_FACTOR * TENSOR_FACTOR, C_Z), TENSOR_FACTOR ** -0.5, 1.0, (), jnp.float32)
    return dict(sequence_matrix=sequence_matrix, pair_representation=pair_representation, alignment_row_mask=alignment_row_mask, residue_mask=residue_mask, attention_scale_vector=attention_scale_vector, asking_factor_matrix=asking_factor_matrix, lookup_factor_matrix=lookup_factor_matrix, content_factor_matrix=content_factor_matrix, sigmoid_factor_matrix=sigmoid_factor_matrix, final_factor_matrix=final_factor_matrix, pair_norm_gain=pair_norm_gain, bias_weight=bias_weight, tensor_scale_vector=tensor_scale_vector, first_factor_matrix=first_factor_matrix, second_factor_matrix=second_factor_matrix, outer_weight=outer_weight)


exact_arithmetic = lax.Precision.HIGHEST

def apply_layer_norm(values, gains):
    center = values - lax.optimization_barrier(jnp.mean(values, axis=-1, keepdims=True))
    spread = lax.optimization_barrier(jnp.mean(center * center, axis=-1, keepdims=True))
    return center * lax.rsqrt(spread + 1e-05) * gains

def reference(sequence_matrix, pair_representation, alignment_row_mask, residue_mask, attention_scale_vector, asking_factor_matrix, lookup_factor_matrix, content_factor_matrix, sigmoid_factor_matrix, final_factor_matrix, pair_norm_gain, bias_weight, tensor_scale_vector, first_factor_matrix, second_factor_matrix, outer_weight):
    split_groups = FEATURE_DEPTH // ATTENTION_GROUPS
    pair_norm = apply_layer_norm(pair_representation, pair_norm_gain)
    bias_all = jnp.einsum('ijc,ch->hij', pair_norm, bias_weight, precision=exact_arithmetic)
    key_bias = (residue_mask.astype(jnp.float32) - 1.0) * 1000000000.0
    stacked_blocks = jnp.stack([asking_factor_matrix, lookup_factor_matrix, content_factor_matrix, sigmoid_factor_matrix], axis=1)
    inv_root = 1.0 / math.sqrt(split_groups)

    def attend_rows(sequence_features):
        normalized_rows = apply_layer_norm(sequence_features, attention_scale_vector)
        projected_rows = jnp.einsum('ic,cfe->ife', normalized_rows, stacked_blocks, precision=exact_arithmetic).reshape(CROP_LENGTH, 4, ATTENTION_GROUPS, split_groups)
        logits = jnp.einsum('ihd,jhd->hij', projected_rows[:, 0], projected_rows[:, 1], precision=exact_arithmetic) * inv_root + bias_all + key_bias
        largest = lax.optimization_barrier(jnp.max(logits, axis=-1, keepdims=True))
        exponent = jnp.exp(logits - largest)
        weights = exponent / lax.optimization_barrier(jnp.sum(exponent, axis=-1, keepdims=True))
        attended = jnp.einsum('hij,jhd->ihd', weights, projected_rows[:, 2], precision=exact_arithmetic)
        sigmoid_scaled = attended * jax.nn.sigmoid(projected_rows[:, 3])
        return sequence_features + jnp.dot(sigmoid_scaled.reshape(CROP_LENGTH, FEATURE_DEPTH), final_factor_matrix, precision=exact_arithmetic)
    alignment_updated = lax.map(attend_rows, sequence_matrix)
    outer_product_norm = apply_layer_norm(alignment_updated, tensor_scale_vector)
    res_live = residue_mask.astype(jnp.float32)
    live = alignment_row_mask.astype(jnp.float32)[:, None] * res_live[None, :]
    left_side = jnp.einsum('sic,co->sio', outer_product_norm, first_factor_matrix, precision=exact_arithmetic) * live[..., None]
    right = jnp.einsum('sic,co->sio', outer_product_norm, second_factor_matrix, precision=exact_arithmetic) * live[..., None]
    count = jnp.sum(alignment_row_mask.astype(jnp.float32))
    row_block_slice = CROP_LENGTH // N_ROW
    left_side_blocks = left_side.reshape(SEQUENCE_TOTAL, N_ROW, row_block_slice, TENSOR_FACTOR).transpose(1, 0, 2, 3)
    live_blocks = res_live.reshape(N_ROW, row_block_slice)

    def outer_block(inputs):
        left_part, live_part = inputs
        outer = jnp.einsum('sic,sjd->ijcd', left_part, right, precision=exact_arithmetic).reshape(row_block_slice, CROP_LENGTH, TENSOR_FACTOR * TENSOR_FACTOR)
        pair_update = jnp.einsum('ijk,kz->ijz', outer, outer_weight, precision=exact_arithmetic)
        norm_function = count * live_part[:, None] * res_live[None, :] + 0.001
        return pair_update / norm_function[..., None]
    pair_updates = lax.map(outer_block, (left_side_blocks, live_blocks)).reshape(CROP_LENGTH, CROP_LENGTH, C_Z)
    return (alignment_updated, pair_representation + pair_updates)
```

```python
import math

import jax
import jax.numpy as jnp
import numpy as np
from jax import lax
from jax.experimental import pallas as pl
from jax.experimental.pallas import tpu as pltpu
from jax.sharding import PartitionSpec as P

exact = lax.Precision.HIGHEST
f32 = jnp.float32
bf16 = jnp.bfloat16
MIB = 1024 * 1024

Z, A, H = 8, 4, 8
STEPS = (16, 8, 4, 2, 1)


def spread_table():
    far = np.zeros((H, H), np.int32)
    ring = lambda d, n: min(d % n, -d % n)
    for c in range(H):
        def plane(h):
            return ring(h // 2 - c // 2, 4) + 2 * ((h ^ c) & 1)

        columns = sorted(range(H), key=lambda h: (-plane(h), (h // 2 - c // 2) % 4))
        planes = sorted(range(Z), key=lambda b: (ring(b - c, Z), (b - c) % Z))
        for h, b in zip(columns, planes):
            far[c][h] = b
    return far


FAR = spread_table()


def reverse_bits(v):
    return int(format(v, "05b")[::-1], 2)


def bias_moves():
    return [
        ((4 * b + a) * H + h, (4 * int(FAR[b][h]) + a) * H + b)
        for b in range(Z)
        for a in range(A)
        for h in range(H)
    ]


def tables():
    bias = np.zeros((Z * A, H, 32), np.int32)
    left = np.zeros((Z * A, H, 32), np.int32)
    for r in range(Z * A):
        for h in range(H):
            for block in range(H):
                for a in range(A):
                    bias[r, h, block * A + a] = reverse_bits(r ^ (4 * int(FAR[h][block]) + a))
            for a in range(A):
                for column in range(H):
                    source = 4 * int(FAR[r // 4][column]) + a
                    left[r, h, a * H + column] = reverse_bits(r ^ source)
    return np.concatenate([bias, left], axis=-1).reshape(Z * A * H, 64)


TABLES = tables()


def gather_row(block):
    for step in STEPS:
        other = lax.ppermute(block, "row", [(r, r ^ step) for r in range(Z * A)])
        block = jnp.concatenate([block, other], axis=0)
    return block


def split(v):
    high = v.astype(bf16)
    return high, (v - high.astype(f32)).astype(bf16)


def dot(a, b, dims=((1,), (0,))):
    return lax.dot_general(a, b, (dims, ((), ())), preferred_element_type=f32)


def dot_exact(a, b, dims=((1,), (0,))):
    return lax.dot_general(a, b, (dims, ((), ())), precision=exact, preferred_element_type=f32)


def norm_rows(v, gain):
    center = v - jnp.mean(v, axis=-1, keepdims=True)
    spread = jnp.mean(center * center, axis=-1, keepdims=True)
    return center * lax.rsqrt(spread + 1e-05) * gain


def bias_kernel(pair_ref, gain_ref, weight_ref, out_ref):
    rows = pair_ref[...].reshape(1024, 128)
    normed = norm_rows(rows, gain_ref[...])
    pick = lax.broadcasted_iota(jnp.int32, (8, 128), 0) == (
        lax.broadcasted_iota(jnp.int32, (8, 128), 1) // 16
    )
    wide = dot_exact(weight_ref[...], jnp.where(pick, 1.0, 0.0))
    result = dot_exact(normed, wide)
    lane = lax.broadcasted_iota(jnp.int32, (64, 128), 1) % 16
    total = jnp.zeros((64, 128), f32)
    for i in range(16):
        total = jnp.where(lane == i, result[64 * i : 64 * i + 64], total)
    out_ref[0] = total


def logits_kernel(
    all_ref, own_ref, gain_ref, wq_ref, wk_ref, wv_ref, wg_ref, logit_ref, vh_ref, vl_ref, gate_ref
):
    gain = gain_ref[...]
    own = norm_rows(own_ref[...].reshape(128, 256), gain)
    query = dot_exact(own, wq_ref[...]) * (1.0 / math.sqrt(32))
    gate_ref[...] = jax.nn.sigmoid(dot_exact(own, wg_ref[...]))
    head_of_lane = lax.broadcasted_iota(jnp.int32, (128, 256), 1) // 32
    head_of_row = lax.broadcasted_iota(jnp.int32, (128, 256), 0) // 16
    keep = head_of_lane == head_of_row
    for s in range(2):
        rows = norm_rows(
            jnp.concatenate([all_ref[b, s] for b in range(8)], axis=0), gain
        )
        keys = dot_exact(rows, wk_ref[...])
        high, low = split(dot_exact(wv_ref[...], rows, ((0,), (1,))))
        vh_ref[s] = high
        vl_ref[s] = low
        spread = []
        for a in range(4):
            part = query[64 * s + 16 * a : 64 * s + 16 * a + 16]
            spread.append(jnp.where(keep, jnp.concatenate([part] * 8, axis=0), 0.0))
        spread = jnp.concatenate(spread, axis=0)
        logit_ref[s] = dot_exact(keys, spread, ((1,), (1,)))


def attend_kernel(
    index_ref,
    bias_ref,
    logit_ref,
    key_ref,
    vh_ref,
    vl_ref,
    gate_ref,
    own_ref,
    wf_ref,
    gain_ref,
    first_ref,
    second_ref,
    live_ref,
    mask_ref,
    msa_ref,
    left_ref,
    right_ref,
    y_ref,
):
    lane = lax.broadcasted_iota(jnp.int32, (32, 128), 1) // 16
    folded = [jnp.zeros((32, 128), f32) for _ in range(8)]
    for s in range(2):
        for a in range(4):
            columns = pl.ds(128 * a, 128)
            tiles = []
            for b in range(8):
                rows = pl.ds(64 * b, 64)
                tiles.append(
                    (logit_ref[s, rows, columns] + bias_ref[index_ref[b * 4 + a]])
                    + key_ref[rows, :]
                )
            logits = jnp.concatenate(tiles, axis=0)
            exponent = jnp.exp(logits - jnp.max(logits, axis=0, keepdims=True))
            weights = exponent / jnp.sum(exponent, axis=0, keepdims=True)
            high, low = split(weights)
            vh = vh_ref[s]
            part = dot(vh, high) + dot(vh, low) + dot(vl_ref[s], high)
            for h in range(8):
                moved = pltpu.roll(
                    part[32 * h : 32 * h + 32], (64 * s + 16 * a - 16 * h) % 128, 1
                )
                folded[h] = jnp.where(lane == 4 * s + a, moved, folded[h])
    attended = jnp.transpose(jnp.concatenate(folded, axis=0)) * gate_ref[...]
    updated = own_ref[...].reshape(128, 256) + dot_exact(attended, wf_ref[...])
    msa_ref[...] = updated.reshape(2, 64, 256)
    y = norm_rows(updated, gain_ref[...]) * live_ref[...]
    right_ref[0, 0:32, :] = dot_exact(second_ref[...], y, ((1,), (1,)))
    right_ref[0, 32:40, :] = mask_ref[...]
    y_ref[...] = dot_exact(y, first_ref[...])
    lane = lax.broadcasted_iota(jnp.int32, (32, 128), 1) // 32
    left = jnp.zeros((32, 128), f32)
    for k in range(4):
        left = jnp.where(lane == k, y_ref[pl.ds(k, 32, stride=4), :], left)
    for s in range(2):
        for a in range(4):
            left_ref[a, 4 * s : 4 * s + 4, :] = left[16 * s + 4 * a : 16 * s + 4 * a + 4]


def outer_kernel(
    index_ref,
    rows_live_ref,
    left_in_ref,
    right_in_ref,
    weight_ref,
    pair_ref,
    cols_live_ref,
    out_ref,
    sorted_ref,
    left_ref,
    right_ref,
):
    for p in range(32):
        spot = pl.multiple_of(index_ref[p] * 8, 8)
        sorted_ref[pl.ds(spot, 8), :] = left_in_ref[p]
    count = jnp.zeros((8, 128), f32)
    for k in range(32):
        count = count + right_in_ref[40 * k + 32 : 40 * k + 40, :]
    count = jnp.sum(count)
    left_rows = []
    for s in range(2):
        left_rows.append(
            jnp.concatenate(
                [sorted_ref[pl.ds(4 * s + q, 32, stride=8), :] for q in range(4)], axis=1
            )
        )
    left = jnp.concatenate(left_rows, axis=0)
    high = left.astype(bf16).astype(f32)
    low = left - high
    left_ref[...] = jnp.transpose(jnp.concatenate([high, high, low, jnp.zeros_like(low)], axis=0)).astype(bf16)
    lane = lax.broadcasted_iota(jnp.int32, (32, 128), 1) < 64
    for d in range(16):
        even = right_in_ref[pl.ds(2 * d, 32, stride=40), :]
        odd = right_in_ref[pl.ds(2 * d + 1, 32, stride=40), :]
        both = jnp.concatenate(
            [
                jnp.where(lane, even, pltpu.roll(odd, 64, 1)),
                jnp.where(lane, pltpu.roll(even, 64, 1), odd),
            ],
            axis=0,
        )
        high, low = split(both)
        columns = pl.ds(128 * d, 128)
        right_ref[0:64, columns] = high
        right_ref[64:128, columns] = low
        right_ref[128:192, columns] = high
        right_ref[192:256, columns] = jnp.zeros((64, 128), bf16)
    weight_high, weight_low = split(weight_ref[...])
    lane = lax.broadcasted_iota(jnp.int32, (128, 128), 1) < 64
    for q in range(8):
        outer = dot(left_ref[64 * q : 64 * q + 64, :], right_ref[...])
        stacked = jnp.concatenate(
            [
                jnp.concatenate(
                    [outer[32 * e : 32 * e + 32, 128 * d : 128 * d + 128] for d in range(16)],
                    axis=0,
                )
                for e in range(2)
            ],
            axis=1,
        )
        high, low = split(stacked)
        y = dot(weight_high, high) + dot(weight_high, low) + dot(weight_low, high)
        top, bottom = y[0:128], y[128:256]
        total = jnp.where(
            lane,
            top[:, 0:128] + pltpu.roll(bottom[:, 0:128], 64, 1),
            pltpu.roll(top[:, 128:256], 64, 1) + bottom[:, 128:256],
        )
        total = jnp.transpose(total)
        for e in range(2):
            i = 2 * q + e
            norm = count * rows_live_ref[i] * cols_live_ref[...] + 0.001
            out_ref[i] = pair_ref[i] + total[64 * e : 64 * e + 64] / norm


def spec(count):
    return [pl.BlockSpec(memory_space=pltpu.VMEM)] * count


def smem(count):
    return [pl.BlockSpec(memory_space=pltpu.SMEM)] * count


def struct(*shape, dtype=f32):
    return jax.ShapeDtypeStruct(shape, dtype)


def call(kernel, numbers, inputs, outputs, scratch=(), limit=48, flops=0, touched=0):
    return pl.pallas_call(
        kernel,
        in_specs=smem(numbers) + spec(inputs),
        out_specs=spec(len(outputs)),
        out_shape=outputs,
        scratch_shapes=list(scratch),
        compiler_params=pltpu.CompilerParams(vmem_limit_bytes=limit * MIB),
        cost_estimate=pl.CostEstimate(flops=flops, bytes_accessed=touched, transcendentals=0),
    )


def body(
    sequence_matrix,
    pair_representation,
    alignment_row_mask,
    residue_mask,
    attention_scale_vector,
    asking_factor_matrix,
    lookup_factor_matrix,
    content_factor_matrix,
    sigmoid_factor_matrix,
    final_factor_matrix,
    pair_norm_gain,
    bias_weight,
    tensor_scale_vector,
    first_factor_matrix,
    second_factor_matrix,
    outer_weight,
):
    head_index = lax.axis_index("head")
    row_index = lax.axis_index("row")
    both = ("row", "head")
    everyone = lax.all_to_all(
        jnp.broadcast_to(sequence_matrix[None], (H, *sequence_matrix.shape)),
        "head",
        0,
        0,
        tiled=True,
    )
    (block,) = call(bias_kernel, 0, 3, [struct(1, 64, 128)], flops=2 * 1024 * 128 * 128 * 6, touched=600000)(
        pair_representation, pair_norm_gain[None], bias_weight
    )
    bias = gather_row(lax.ppermute(block, both, bias_moves()))

    residue_live = residue_mask.astype(f32)
    key_bias = jnp.broadcast_to(((residue_live - 1.0) * 1000000000.0)[:, None], (512, 128))
    cols_live = lax.dynamic_slice_in_dim(residue_live, head_index * 64, 64)
    rows_live = lax.dynamic_slice_in_dim(residue_live, row_index * 16, 16)
    row_live = alignment_row_mask.astype(f32)
    live = (row_live[:, None] * cols_live[None, :]).reshape(128, 1)
    mask_tile = jnp.zeros((8, 128), f32).at[0, 0:2].set(row_live)
    device_tables = lax.dynamic_index_in_dim(
        jnp.asarray(TABLES), row_index * H + head_index, 0, keepdims=False
    )
    weight = (
        outer_weight.reshape(32, 16, 2, 128).transpose(2, 3, 1, 0).reshape(256, 512)
    )

    logits, vh, vl, gate = call(
        logits_kernel,
        0,
        7,
        [
            struct(2, 512, 512),
            struct(2, 256, 512, dtype=bf16),
            struct(2, 256, 512, dtype=bf16),
            struct(128, 256),
        ],
        flops=6 * 2 * 1024 * 256 * 1024,
        touched=6 * MIB,
    )(
        everyone,
        sequence_matrix,
        attention_scale_vector[None],
        asking_factor_matrix,
        lookup_factor_matrix,
        content_factor_matrix,
        sigmoid_factor_matrix,
    )
    msa_out, left, right = call(
        attend_kernel,
        1,
        13,
        [struct(2, 64, 256), struct(4, 8, 128), struct(1, 40, 128)],
        scratch=[pltpu.VMEM((128, 128), f32)],
        flops=3 * 2 * 1024 * 512 * 256,
        touched=6 * MIB,
    )(
        device_tables[0:32],
        bias,
        logits,
        key_bias,
        vh,
        vl,
        gate,
        sequence_matrix,
        final_factor_matrix,
        tensor_scale_vector[None],
        jnp.tile(first_factor_matrix, (1, 4)),
        second_factor_matrix.T,
        live,
        mask_tile,
    )
    left = lax.ppermute(left, both, [(d, s) for s, d in bias_moves()])
    right = gather_row(right)
    left = lax.all_to_all(
        jnp.broadcast_to(left[:, None], (A, H, 8, 128)).reshape(A * H, 8, 128),
        both,
        0,
        0,
        tiled=True,
        axis_index_groups=[[32 * z + k for k in range(32)] for z in range(Z)],
    )
    (pair_out,) = call(
        outer_kernel,
        2,
        5,
        [struct(16, 64, 128)],
        scratch=[
            pltpu.VMEM((256, 128), f32),
            pltpu.VMEM((512, 256), bf16),
            pltpu.VMEM((256, 2048), bf16),
        ],
        flops=3 * 2 * 1024 * 1024 * 256,
        touched=4 * MIB,
    )(
        device_tables[32:64],
        rows_live,
        left,
        right.reshape(32 * 40, 128),
        weight,
        pair_representation,
        cols_live[:, None],
    )
    return msa_out, pair_out


def solution(mesh):
    cells = P("row", "head", None)
    return jax.shard_map(
        body,
        mesh=mesh,
        in_specs=(cells, cells, P("row")) + (P(),) * 13,
        out_specs=(cells, cells),
        check_vma=False,
    )
```

```python
import math

import jax
import jax.numpy as jnp
import numpy as np
from jax import lax
from jax.experimental import pallas as pl
from jax.experimental.pallas import tpu as pltpu
from jax.sharding import PartitionSpec as P

exact = lax.Precision.HIGHEST
f32 = jnp.float32
bf16 = jnp.bfloat16
MIB = 1024 * 1024

Z, A, H = 8, 4, 8
def spread_table():
    far = np.zeros((H, H), np.int32)
    ring = lambda d, n: min(d % n, -d % n)
    for c in range(H):
        def plane(h):
            return ring(h // 2 - c // 2, 4) + 2 * ((h ^ c) & 1)

        columns = sorted(range(H), key=lambda h: (-plane(h), (h // 2 - c // 2) % 4))
        planes = sorted(range(Z), key=lambda b: (ring(b - c, Z), (b - c) % Z))
        for h, b in zip(columns, planes):
            far[c][h] = b
    return far


FAR = spread_table()


def bias_moves():
    return [
        ((4 * b + a) * H + h, (4 * int(FAR[b][h]) + a) * H + b)
        for b in range(Z)
        for a in range(A)
        for h in range(H)
    ]


def from_plane(v, far):
    return lax.ppermute(v, "row", [(r, (r - 4 * far) % 32) for r in range(Z * A)])


def from_neighbour(v, bit):
    return lax.ppermute(v, "row", [(r, r ^ bit) for r in range(Z * A)])


def gather_row(own, before_far=None, before_side=None):
    near = jnp.concatenate([from_plane(own, -1), own, from_plane(own, 1)], axis=0)
    if before_far is not None:
        near = lax.optimization_barrier((near, before_far))[0]
    pieces = [near, from_plane(near, 3), from_plane(near[1:3], -3)]
    if before_side is not None:
        pieces = list(lax.optimization_barrier((*pieces, before_side)))[:3]
    sides = [from_neighbour(p, 2) for p in pieces]
    return (
        pieces
        + [from_neighbour(p, 1) for p in pieces]
        + sides
        + [from_neighbour(p, 1) for p in sides]
    )


SIZES = (3, 3, 2) * 4
STARTS = tuple(sum(SIZES[:k]) for k in range(12))


def position(row, source_plane, source_side):
    side = jnp.bitwise_xor(jnp.bitwise_and(row, 3), source_side)
    plane = jnp.bitwise_and(source_plane - jnp.right_shift(row, 2) + 1, 7)
    return side * 8 + plane


def split(v):
    high = v.astype(bf16)
    return high, (v - high.astype(f32)).astype(bf16)


def dot(a, b, dims=((1,), (0,))):
    return lax.dot_general(a, b, (dims, ((), ())), preferred_element_type=f32)


def dot_exact(a, b, dims=((1,), (0,))):
    return lax.dot_general(a, b, (dims, ((), ())), precision=exact, preferred_element_type=f32)


def norm_rows(v, gain):
    center = v - jnp.mean(v, axis=-1, keepdims=True)
    spread = jnp.mean(center * center, axis=-1, keepdims=True)
    return center * lax.rsqrt(spread + 1e-05) * gain


def bias_kernel(pair_ref, gain_ref, weight_ref, own_ref, out_ref, copies_ref, sems):
    copies = [
        pltpu.make_async_copy(own_ref, copies_ref.at[k], sems.at[k]) for k in range(H)
    ]
    for copy in copies:
        copy.start()
    rows = pair_ref[...].reshape(1024, 128)
    normed = norm_rows(rows, gain_ref[...])
    pick = lax.broadcasted_iota(jnp.int32, (8, 128), 0) == (
        lax.broadcasted_iota(jnp.int32, (8, 128), 1) // 16
    )
    wide = dot_exact(weight_ref[...], jnp.where(pick, 1.0, 0.0), ((0,), (0,)))
    result = dot_exact(normed, wide)
    lane = lax.broadcasted_iota(jnp.int32, (64, 128), 1) % 16
    total = jnp.zeros((64, 128), f32)
    for i in range(16):
        total = jnp.where(lane == i, result[64 * i : 64 * i + 64], total)
    out_ref[0] = total
    for copy in copies:
        copy.wait()


def logits_kernel(
    all_ref, own_ref, gain_ref, wq_ref, wk_ref, wv_ref, wg_ref, logit_ref, vh_ref, vl_ref, gate_ref
):
    gain = gain_ref[...]
    own = norm_rows(own_ref[...].reshape(128, 256), gain)
    query = dot_exact(own, wq_ref[...]) * (1.0 / math.sqrt(32))
    gate_ref[...] = jax.nn.sigmoid(dot_exact(own, wg_ref[...]))
    head_of_lane = lax.broadcasted_iota(jnp.int32, (128, 256), 1) // 32
    head_of_row = lax.broadcasted_iota(jnp.int32, (128, 256), 0) // 16
    keep = head_of_lane == head_of_row
    for s in range(2):
        rows = norm_rows(
            jnp.concatenate([all_ref[b, s] for b in range(8)], axis=0), gain
        )
        keys = dot_exact(rows, wk_ref[...])
        high, low = split(dot_exact(wv_ref[...], rows, ((0,), (1,))))
        vh_ref[s] = high
        vl_ref[s] = low
        spread = []
        for a in range(4):
            part = query[64 * s + 16 * a : 64 * s + 16 * a + 16]
            spread.append(jnp.where(keep, jnp.concatenate([part] * 8, axis=0), 0.0))
        spread = jnp.concatenate(spread, axis=0)
        logit_ref[s] = dot_exact(keys, spread, ((1,), (1,)))


def attend_kernel(
    far_ref,
    *refs,
):
    attend(far_ref, refs[:12], *refs[12:])


def attend(
    far_ref,
    piece_refs,
    logit_ref,
    key_ref,
    vh_ref,
    vl_ref,
    gate_ref,
    own_ref,
    wf_ref,
    gain_ref,
    first_ref,
    second_ref,
    live_ref,
    mask_ref,
    msa_ref,
    left_ref,
    right_ref,
    bias_ref,
    y_ref,
):
    for piece_ref, start, size in zip(piece_refs, STARTS, SIZES):
        bias_ref[start : start + size] = piece_ref[...]
    row = lax.axis_index("row")
    column = lax.axis_index("head")
    lane = lax.broadcasted_iota(jnp.int32, (32, 128), 1) // 16
    folded = [jnp.zeros((32, 128), f32) for _ in range(8)]
    for s in range(2):
        for a in range(4):
            columns = pl.ds(128 * a, 128)
            tiles = []
            for b in range(8):
                rows = pl.ds(64 * b, 64)
                tiles.append(
                    (logit_ref[s, rows, columns] + bias_ref[position(row, far_ref[column * H + b], a)])
                    + key_ref[rows, :]
                )
            logits = jnp.concatenate(tiles, axis=0)
            exponent = jnp.exp(logits - jnp.max(logits, axis=0, keepdims=True))
            weights = exponent / jnp.sum(exponent, axis=0, keepdims=True)
            high, low = split(weights)
            vh = vh_ref[s]
            part = dot(vh, high) + dot(vh, low) + dot(vl_ref[s], high)
            for h in range(8):
                moved = pltpu.roll(
                    part[32 * h : 32 * h + 32], (64 * s + 16 * a - 16 * h) % 128, 1
                )
                folded[h] = jnp.where(lane == 4 * s + a, moved, folded[h])
    attended = jnp.transpose(jnp.concatenate(folded, axis=0)) * gate_ref[...]
    updated = own_ref[...].reshape(128, 256) + dot_exact(attended, wf_ref[...])
    msa_ref[...] = updated.reshape(2, 64, 256)
    y = norm_rows(updated, gain_ref[...]) * live_ref[...]
    right_ref[0, 0:32, :] = dot_exact(second_ref[...], y, ((1,), (1,)))
    right_ref[0, 32:40, :] = mask_ref[...]
    y_ref[...] = dot_exact(y, first_ref[...])
    lane = lax.broadcasted_iota(jnp.int32, (32, 128), 1) // 32
    left = jnp.zeros((32, 128), f32)
    for k in range(4):
        left = jnp.where(lane == k, y_ref[pl.ds(k, 32, stride=4), :], left)
    for s in range(2):
        for a in range(4):
            left_ref[a, 4 * s : 4 * s + 4, :] = left[16 * s + 4 * a : 16 * s + 4 * a + 4]


def outer_kernel(
    far_ref,
    rows_live_ref,
    *refs,
):
    outer_product(far_ref, rows_live_ref, refs[:12], *refs[12:])


def outer_product(
    far_ref,
    rows_live_ref,
    piece_refs,
    left_in_ref,
    weight_ref,
    pair_ref,
    cols_live_ref,
    out_ref,
    right_in_ref,
    sorted_ref,
    left_ref,
    right_ref,
):
    for piece_ref, start, size in zip(piece_refs, STARTS, SIZES):
        for k in range(size):
            right_in_ref[40 * (start + k) : 40 * (start + k) + 40, :] = piece_ref[k]
    row = lax.axis_index("row")
    for p in range(32):
        source = position(row, far_ref[jnp.right_shift(row, 2) * H + p % H], p // H)
        spot = pl.multiple_of(source * 8, 8)
        sorted_ref[pl.ds(spot, 8), :] = left_in_ref[p]
    count = jnp.zeros((8, 128), f32)
    for k in range(32):
        count = count + right_in_ref[40 * k + 32 : 40 * k + 40, :]
    count = jnp.sum(count)
    left_rows = []
    for s in range(2):
        left_rows.append(
            jnp.concatenate(
                [sorted_ref[pl.ds(4 * s + q, 32, stride=8), :] for q in range(4)], axis=1
            )
        )
    left = jnp.concatenate(left_rows, axis=0)
    high = left.astype(bf16).astype(f32)
    low = left - high
    left_ref[...] = jnp.transpose(jnp.concatenate([high, high, low, jnp.zeros_like(low)], axis=0)).astype(bf16)
    lane = lax.broadcasted_iota(jnp.int32, (32, 128), 1) < 64
    for d in range(16):
        even = right_in_ref[pl.ds(2 * d, 32, stride=40), :]
        odd = right_in_ref[pl.ds(2 * d + 1, 32, stride=40), :]
        both = jnp.concatenate(
            [
                jnp.where(lane, even, pltpu.roll(odd, 64, 1)),
                jnp.where(lane, pltpu.roll(even, 64, 1), odd),
            ],
            axis=0,
        )
        high, low = split(both)
        columns = pl.ds(128 * d, 128)
        right_ref[0:64, columns] = high
        right_ref[64:128, columns] = low
        right_ref[128:192, columns] = high
        right_ref[192:256, columns] = jnp.zeros((64, 128), bf16)
    weight_high, weight_low = split(weight_ref[...])
    lane = lax.broadcasted_iota(jnp.int32, (128, 128), 1) < 64
    for q in range(8):
        outer = dot(left_ref[64 * q : 64 * q + 64, :], right_ref[...])
        stacked = jnp.concatenate(
            [
                jnp.concatenate(
                    [outer[32 * e : 32 * e + 32, 128 * d : 128 * d + 128] for d in range(16)],
                    axis=0,
                )
                for e in range(2)
            ],
            axis=1,
        )
        high, low = split(stacked)
        y = dot(weight_high, high) + dot(weight_high, low) + dot(weight_low, high)
        top, bottom = y[0:128], y[128:256]
        total = jnp.where(
            lane,
            top[:, 0:128] + pltpu.roll(bottom[:, 0:128], 64, 1),
            pltpu.roll(top[:, 128:256], 64, 1) + bottom[:, 128:256],
        )
        total = jnp.transpose(total)
        for e in range(2):
            i = 2 * q + e
            norm = count * rows_live_ref[i] * cols_live_ref[...] + 0.001
            out_ref[i] = pair_ref[i] + total[64 * e : 64 * e + 64] / norm


def vmem(count):
    return [pl.BlockSpec(memory_space=pltpu.VMEM)] * count


def smem(count):
    return [pl.BlockSpec(memory_space=pltpu.SMEM)] * count


def anywhere(count):
    return [pl.BlockSpec(memory_space=pl.ANY)] * count


def struct(*shape, dtype=f32):
    return jax.ShapeDtypeStruct(shape, dtype)


def call(kernel, inputs, outputs, shapes, scratch=(), limit=48, flops=0, touched=0):
    return pl.pallas_call(
        kernel,
        in_specs=inputs,
        out_specs=outputs,
        out_shape=shapes,
        scratch_shapes=list(scratch),
        compiler_params=pltpu.CompilerParams(vmem_limit_bytes=limit * MIB),
        cost_estimate=pl.CostEstimate(flops=flops, bytes_accessed=touched, transcendentals=0),
    )


def body(
    sequence_matrix,
    pair_representation,
    alignment_row_mask,
    residue_mask,
    attention_scale_vector,
    asking_factor_matrix,
    lookup_factor_matrix,
    content_factor_matrix,
    sigmoid_factor_matrix,
    final_factor_matrix,
    pair_norm_gain,
    bias_weight,
    tensor_scale_vector,
    first_factor_matrix,
    second_factor_matrix,
    outer_weight,
):
    head_index = lax.axis_index("head")
    row_index = lax.axis_index("row")
    both = ("row", "head")
    block, copies = call(
        bias_kernel,
        vmem(3) + anywhere(1),
        vmem(1) + anywhere(1),
        [struct(1, 64, 128), struct(H, 2, 64, 256)],
        scratch=[pltpu.SemaphoreType.DMA((H,))],
        flops=2 * 1024 * 128 * 128 * 6,
        touched=600000,
    )(pair_representation, pair_norm_gain[None], bias_weight.T, sequence_matrix)
    everyone = lax.all_to_all(copies, "head", 0, 0, tiled=True)
    bias = gather_row(lax.ppermute(block, both, bias_moves()))

    residue_live = residue_mask.astype(f32)
    key_bias = jnp.broadcast_to(((residue_live - 1.0) * 1000000000.0)[:, None], (512, 128))
    cols_live = lax.dynamic_slice_in_dim(residue_live, head_index * 64, 64)
    rows_live = lax.dynamic_slice_in_dim(residue_live, row_index * 16, 16)
    row_live = alignment_row_mask.astype(f32)
    live = (row_live[:, None] * cols_live[None, :]).reshape(128, 1)
    mask_tile = jnp.zeros((8, 128), f32).at[0, 0:2].set(row_live)
    far = jnp.asarray(FAR.reshape(-1))
    weight = (
        outer_weight.reshape(32, 16, 2, 128).transpose(2, 3, 1, 0).reshape(256, 512)
    )

    logits, vh, vl, gate = call(
        logits_kernel,
        vmem(7),
        vmem(4),
        [
            struct(2, 512, 512),
            struct(2, 256, 512, dtype=bf16),
            struct(2, 256, 512, dtype=bf16),
            struct(128, 256),
        ],
        flops=6 * 2 * 1024 * 256 * 1024,
        touched=6 * MIB,
    )(
        everyone,
        sequence_matrix,
        attention_scale_vector[None],
        asking_factor_matrix,
        lookup_factor_matrix,
        content_factor_matrix,
        sigmoid_factor_matrix,
    )
    msa_out, left, right = call(
        attend_kernel,
        smem(1) + vmem(24),
        vmem(3),
        [struct(2, 64, 256), struct(4, 8, 128), struct(1, 40, 128)],
        scratch=[pltpu.VMEM((32, 64, 128), f32), pltpu.VMEM((128, 128), f32)],
        flops=3 * 2 * 1024 * 512 * 256,
        touched=6 * MIB,
    )(
        far,
        *bias,
        logits,
        key_bias,
        vh,
        vl,
        gate,
        sequence_matrix,
        final_factor_matrix,
        tensor_scale_vector[None],
        jnp.tile(first_factor_matrix, (1, 4)),
        second_factor_matrix.T,
        live,
        mask_tile,
    )
    left = lax.ppermute(left, both, [(d, s) for s, d in bias_moves()])
    arrived = left
    left = lax.all_to_all(
        jnp.broadcast_to(left[:, None], (A, H, 8, 128)).reshape(A * H, 8, 128),
        both,
        0,
        0,
        tiled=True,
        axis_index_groups=[[32 * z + k for k in range(32)] for z in range(Z)],
    )
    right = gather_row(right, arrived, left)
    (pair_out,) = call(
        outer_kernel,
        smem(2) + vmem(16),
        vmem(1),
        [struct(16, 64, 128)],
        scratch=[
            pltpu.VMEM((1280, 128), f32),
            pltpu.VMEM((256, 128), f32),
            pltpu.VMEM((512, 256), bf16),
            pltpu.VMEM((256, 2048), bf16),
        ],
        flops=3 * 2 * 1024 * 1024 * 256,
        touched=4 * MIB,
    )(
        far,
        rows_live,
        *right,
        left,
        weight,
        pair_representation,
        cols_live[:, None],
    )
    return msa_out, pair_out


def solution(mesh):
    cells = P("row", "head", None)
    return jax.shard_map(
        body,
        mesh=mesh,
        in_specs=(cells, cells, P("row")) + (P(),) * 13,
        out_specs=(cells, cells),
        check_vma=False,
    )
```

```python
import itertools
import math

import jax
import jax.numpy as jnp
import numpy as np
from jax import lax
from jax.experimental import pallas as pl
from jax.experimental.pallas import tpu as pltpu
from jax.sharding import PartitionSpec as P

exact = lax.Precision.HIGHEST
f32 = jnp.float32
bf16 = jnp.bfloat16
MIB = 1024 * 1024

Z, A, H = 8, 4, 8
def ring(d, n):
    return min(d % n, -d % n)


def spread_tables():
    once = np.zeros((H, H), np.int32)
    twice = np.zeros((H, 2, H), np.int32)
    for c in range(H):
        hops = [
            [ring(h // 2 - c // 2, 4) + 2 * ((h ^ c) & 1) + ring(b - c, Z) for b in range(Z)]
            for h in range(H)
        ]
        flat = [hops[h][c] for h in range(H)]
        columns = sorted(range(H), key=lambda h: (-flat[h], h))
        planes = sorted(range(Z), key=lambda b: (ring(b - c, Z), (b - c) % Z))
        for h, b in zip(columns, planes):
            once[c][h] = b

        def fit(group, half):
            return min(
                (
                    (max(hops[h][b] for h, b in zip(group, p)), sum(hops[h][b] for h, b in zip(group, p)), p)
                    for p in itertools.permutations(range(4 * half, 4 * half + 4))
                )
            )

        best = None
        for low in itertools.combinations(range(H), 4):
            high = tuple(h for h in range(H) if h not in low)
            first = fit(low, 0), fit(high, 1)
            second = fit(low, 1), fit(high, 0)
            cost = (
                max(first[0][0], first[1][0]) + max(second[0][0], second[1][0]),
                sum(f[1] for f in first + second),
            )
            if best is None or cost < best[0]:
                best = cost, low, high, first, second
        _, low, high, first, second = best
        for k, fits in enumerate((first, second)):
            for group, found in zip((low, high), fits):
                for h, b in zip(group, found[2]):
                    twice[c][k][h] = b
    return once, twice


ONCE, TWICE = spread_tables()


def moves(table):
    return [
        ((4 * b + a) * H + h, (4 * int(table[b][h]) + a) * H + b)
        for b in range(Z)
        for a in range(A)
        for h in range(H)
    ]


def spots():
    out = np.zeros((H, 2, H), np.int32)
    for c in range(H):
        for k in range(2):
            for h in range(H):
                plane = int(TWICE[c][k][h])
                out[c][plane // 4][h] = 4 * k + plane % 4
    return out


SPOTS = spots()


def from_neighbour(v, bit):
    return lax.ppermute(v, "row", [(r, r ^ bit) for r in range(Z * A)])


def after(values, *others):
    return list(lax.optimization_barrier((*values, *others)))[: len(values)]


def gather_halves(first, second):
    own = jnp.concatenate([first, second], axis=0)
    near = jnp.concatenate([own, from_neighbour(own, 8)], axis=0)
    return [near, from_neighbour(near, 4)]


def gather_sides(pieces):
    return [from_neighbour(p, 2) for p in pieces]


def gather_cores(pieces, sides):
    return (
        pieces
        + [from_neighbour(p, 1) for p in pieces]
        + sides
        + [from_neighbour(p, 1) for p in sides]
    )


def side_of(row, source_side):
    return jnp.bitwise_xor(jnp.bitwise_and(row, 3), source_side) * 8


def half_position(row, spot, source_side):
    plane = jnp.bitwise_xor(jnp.bitwise_and(jnp.right_shift(row, 2), 3), jnp.bitwise_and(spot, 3))
    return (
        side_of(row, source_side)
        + jnp.bitwise_and(plane, 1) * 4
        + jnp.bitwise_and(plane, 2)
        + jnp.right_shift(spot, 2)
    )


def split(v):
    high = v.astype(bf16)
    return high, (v - high.astype(f32)).astype(bf16)


def dot(a, b, dims=((1,), (0,))):
    return lax.dot_general(a, b, (dims, ((), ())), preferred_element_type=f32)


def dot_exact(a, b, dims=((1,), (0,))):
    return lax.dot_general(a, b, (dims, ((), ())), precision=exact, preferred_element_type=f32)


def three(a, b, dims=((1,), (0,))):
    return dot(a[0], b[0], dims) + (dot(a[0], b[1], dims) + dot(a[1], b[0], dims))


def dot_three(a, b, dims=((1,), (0,))):
    return three(split(a), split(b), dims)


def norm_rows(v, gain):
    center = v - jnp.mean(v, axis=-1, keepdims=True)
    spread = jnp.mean(center * center, axis=-1, keepdims=True)
    return center * lax.rsqrt(spread + 1e-05) * gain


def start_all(copies):
    for copy in copies:
        copy.start()
    return copies


def wait_all(copies):
    for copy in copies:
        copy.wait()


def bias_kernel(
    pair_hbm,
    gain_hbm,
    weight_hbm,
    own_hbm,
    out_ref,
    copies_hbm,
    pair_ref,
    gain_ref,
    weight_ref,
    own_ref,
    sems,
):
    own_load = start_all([pltpu.make_async_copy(own_hbm, own_ref, sems.at[11])])
    loads = start_all(
        [
            pltpu.make_async_copy(gain_hbm, gain_ref, sems.at[8]),
            pltpu.make_async_copy(weight_hbm, weight_ref, sems.at[9]),
            pltpu.make_async_copy(pair_hbm, pair_ref, sems.at[10]),
        ]
    )
    wait_all(own_load)
    copies = start_all(
        [pltpu.make_async_copy(own_ref, copies_hbm.at[k], sems.at[k]) for k in range(H)]
    )
    wait_all(loads)
    rows = pair_ref[...].reshape(1024, 128)
    normed = norm_rows(rows, gain_ref[...])
    pick = lax.broadcasted_iota(jnp.int32, (8, 128), 0) == (
        lax.broadcasted_iota(jnp.int32, (8, 128), 1) // 16
    )
    wide = dot_exact(weight_ref[...], jnp.where(pick, 1.0, 0.0), ((0,), (0,)))
    result = dot_exact(normed, wide)
    lane = lax.broadcasted_iota(jnp.int32, (64, 128), 1) % 16
    total = jnp.zeros((64, 128), f32)
    for i in range(16):
        total = jnp.where(lane == i, result[64 * i : 64 * i + 64], total)
    out_ref[0] = total
    wait_all(copies)


def spread_kernel(left_ref, out_ref, sems):
    wait_all(
        start_all(
            [pltpu.make_async_copy(left_ref, out_ref.at[:, k], sems.at[k]) for k in range(H)]
        )
    )


def logits_kernel(
    all_ref, own_ref, gain_ref, wq_ref, wk_ref, wv_ref, wg_ref, logit_ref, value_ref, gate_ref
):
    gain = gain_ref[...]
    own = split(norm_rows(own_ref[...].reshape(128, 256), gain))
    query = three(own, split(wq_ref[...])) * (1.0 / math.sqrt(32))
    gate_ref[...] = jax.nn.sigmoid(three(own, split(wg_ref[...])))
    head_of_lane = lax.broadcasted_iota(jnp.int32, (128, 256), 1) // 32
    head_of_row = lax.broadcasted_iota(jnp.int32, (128, 256), 0) // 16
    keep = head_of_lane == head_of_row
    key_factor = split(wk_ref[...])
    value_factor = split(jnp.transpose(wv_ref[...]))
    for s in range(2):
        rows = split(
            norm_rows(jnp.concatenate([all_ref[b, s] for b in range(8)], axis=0), gain)
        )
        keys = split(three(rows, key_factor))
        value_ref[0, s], value_ref[1, s] = split(three(value_factor, rows, ((1,), (1,))))
        wide = []
        for a in range(4):
            part = query[64 * s + 16 * a : 64 * s + 16 * a + 16]
            wide.append(jnp.where(keep, jnp.concatenate([part] * 8, axis=0), 0.0))
        logit_ref[s] = three(keys, split(jnp.concatenate(wide, axis=0)), ((1,), (1,)))


def attend_kernel(
    spot_ref,
    *refs,
):
    attend(spot_ref, refs[:8], *refs[8:])


def attend(
    spot_ref,
    piece_refs,
    logit_ref,
    key_ref,
    value_ref,
    gate_ref,
    own_ref,
    wf_ref,
    gain_ref,
    first_ref,
    second_ref,
    live_ref,
    mask_ref,
    msa_ref,
    left_ref,
    right_ref,
    bias_ref,
    y_ref,
):
    for k, piece_ref in enumerate(piece_refs):
        bias_ref[4 * k : 4 * k + 4] = piece_ref[...]
    row = lax.axis_index("row")
    spots_at = (lax.axis_index("head") * 2 + jnp.right_shift(row, 4)) * H
    lane = lax.broadcasted_iota(jnp.int32, (32, 128), 1) // 16
    folded = [jnp.zeros((32, 128), f32) for _ in range(8)]
    for s in range(2):
        for a in range(4):
            columns = pl.ds(128 * a, 128)
            tiles = []
            for b in range(8):
                rows = pl.ds(64 * b, 64)
                tiles.append(
                    (logit_ref[s, rows, columns] + bias_ref[half_position(row, spot_ref[spots_at + b], a)])
                    + key_ref[rows, :]
                )
            logits = jnp.concatenate(tiles, axis=0)
            exponent = jnp.exp(logits - jnp.max(logits, axis=0, keepdims=True))
            weights = exponent * (1.0 / jnp.sum(exponent, axis=0, keepdims=True))
            part = three((value_ref[0, s], value_ref[1, s]), split(weights))
            for h in range(8):
                moved = pltpu.roll(
                    part[32 * h : 32 * h + 32], (64 * s + 16 * a - 16 * h) % 128, 1
                )
                folded[h] = jnp.where(lane == 4 * s + a, moved, folded[h])
    attended = jnp.transpose(jnp.concatenate(folded, axis=0)) * gate_ref[...]
    updated = own_ref[...].reshape(128, 256) + dot_three(attended, wf_ref[...])
    msa_ref[...] = updated.reshape(2, 64, 256)
    y = norm_rows(updated, gain_ref[...]) * live_ref[...]
    y = split(y)
    right = three(split(second_ref[...]), y, ((1,), (1,)))
    for k in range(Z):
        right_ref[k, 0:32, :] = right
        right_ref[k, 32:40, :] = mask_ref[...]
    y_ref[...] = three(y, split(first_ref[...]))
    lane = lax.broadcasted_iota(jnp.int32, (32, 128), 1) // 32
    left = jnp.zeros((32, 128), f32)
    for k in range(4):
        left = jnp.where(lane == k, y_ref[pl.ds(k, 32, stride=4), :], left)
    for s in range(2):
        for a in range(4):
            left_ref[a, 4 * s : 4 * s + 4, :] = left[16 * s + 4 * a : 16 * s + 4 * a + 4]


def outer_kernel(
    once_ref,
    rows_live_ref,
    *refs,
):
    outer_product(once_ref, rows_live_ref, refs[:4], *refs[4:])


def outer_product(
    once_ref,
    rows_live_ref,
    piece_refs,
    left_in_ref,
    weight_ref,
    pair_ref,
    cols_live_ref,
    out_ref,
    right_in_ref,
    sorted_ref,
    left_ref,
    right_ref,
):
    for q, piece_ref in enumerate(piece_refs):
        for k in range(Z):
            start = 40 * (Z * q + k)
            right_in_ref[start : start + 40, :] = piece_ref[k]
    row = lax.axis_index("row")
    for p in range(32):
        source = side_of(row, p // H) + once_ref[jnp.right_shift(row, 2) * H + p % H]
        spot = pl.multiple_of(source * 8, 8)
        sorted_ref[pl.ds(spot, 8), :] = left_in_ref[p]
    count = jnp.zeros((8, 128), f32)
    for k in range(32):
        count = count + right_in_ref[40 * k + 32 : 40 * k + 40, :]
    count = jnp.sum(count)
    left_rows = []
    for s in range(2):
        left_rows.append(
            jnp.concatenate(
                [sorted_ref[pl.ds(4 * s + q, 32, stride=8), :] for q in range(4)], axis=1
            )
        )
    left = jnp.concatenate(left_rows, axis=0)
    high = left.astype(bf16).astype(f32)
    low = left - high
    left_ref[...] = jnp.transpose(jnp.concatenate([high, high, low, jnp.zeros_like(low)], axis=0)).astype(bf16)
    lane = lax.broadcasted_iota(jnp.int32, (32, 128), 1) < 64
    for d in range(16):
        even = right_in_ref[pl.ds(2 * d, 32, stride=40), :]
        odd = right_in_ref[pl.ds(2 * d + 1, 32, stride=40), :]
        both = jnp.concatenate(
            [
                jnp.where(lane, even, pltpu.roll(odd, 64, 1)),
                jnp.where(lane, pltpu.roll(even, 64, 1), odd),
            ],
            axis=0,
        )
        high, low = split(both)
        columns = pl.ds(128 * d, 128)
        right_ref[0:64, columns] = high
        right_ref[64:128, columns] = low
        right_ref[128:192, columns] = high
        right_ref[192:256, columns] = jnp.zeros((64, 128), bf16)
    columns = [
        jnp.concatenate(
            [weight_ref[pl.ds(2 * d + e, 32, stride=32), :] for d in range(16)], axis=0
        )
        for e in range(2)
    ]
    weight = split(jnp.transpose(jnp.concatenate(columns, axis=1)))
    lane = lax.broadcasted_iota(jnp.int32, (128, 128), 1) < 64
    for q in range(8):
        outer = dot(left_ref[64 * q : 64 * q + 64, :], right_ref[...])
        stacked = jnp.concatenate(
            [
                jnp.concatenate(
                    [outer[32 * e : 32 * e + 32, 128 * d : 128 * d + 128] for d in range(16)],
                    axis=0,
                )
                for e in range(2)
            ],
            axis=1,
        )
        y = three(weight, split(stacked))
        top, bottom = y[0:128], y[128:256]
        total = jnp.where(
            lane,
            top[:, 0:128] + pltpu.roll(bottom[:, 0:128], 64, 1),
            pltpu.roll(top[:, 128:256], 64, 1) + bottom[:, 128:256],
        )
        total = jnp.transpose(total)
        for e in range(2):
            i = 2 * q + e
            norm = count * rows_live_ref[i] * cols_live_ref[...] + 0.001
            out_ref[i] = pair_ref[i] + total[64 * e : 64 * e + 64] / norm


def vmem(count):
    return [pl.BlockSpec(memory_space=pltpu.VMEM)] * count


def smem(count):
    return [pl.BlockSpec(memory_space=pltpu.SMEM)] * count


def hbm(count):
    return [pl.BlockSpec(memory_space=pltpu.HBM)] * count


def struct(*shape, dtype=f32):
    return jax.ShapeDtypeStruct(shape, dtype)


def call(kernel, inputs, outputs, shapes, scratch=(), limit=32, flops=0, touched=0):
    return pl.pallas_call(
        kernel,
        in_specs=inputs,
        out_specs=outputs,
        out_shape=shapes,
        scratch_shapes=list(scratch),
        compiler_params=pltpu.CompilerParams(vmem_limit_bytes=limit * MIB),
        cost_estimate=pl.CostEstimate(flops=flops, bytes_accessed=touched, transcendentals=0),
    )


def body(
    sequence_matrix,
    pair_representation,
    alignment_row_mask,
    residue_mask,
    attention_scale_vector,
    asking_factor_matrix,
    lookup_factor_matrix,
    content_factor_matrix,
    sigmoid_factor_matrix,
    final_factor_matrix,
    pair_norm_gain,
    bias_weight,
    tensor_scale_vector,
    first_factor_matrix,
    second_factor_matrix,
    outer_weight,
):
    head_index = lax.axis_index("head")
    row_index = lax.axis_index("row")
    both = ("row", "head")
    block, copies = call(
        bias_kernel,
        hbm(4),
        vmem(1) + hbm(1),
        [struct(1, 64, 128), struct(H, 2, 64, 256)],
        scratch=[
            pltpu.VMEM((16, 64, 128), f32),
            pltpu.VMEM((1, 128), f32),
            pltpu.VMEM((8, 128), f32),
            pltpu.VMEM((2, 64, 256), f32),
            pltpu.SemaphoreType.DMA((H + 4,)),
        ],
        limit=60,
        flops=2 * 1024 * 128 * 128 * 6,
        touched=600000,
    )(pair_representation, pair_norm_gain[None], bias_weight.T, sequence_matrix)
    everyone = lax.all_to_all(copies, "head", 0, 0, tiled=True)
    pieces = gather_halves(
        lax.ppermute(block, both, moves(TWICE[:, 0])), lax.ppermute(block, both, moves(TWICE[:, 1]))
    )
    bias = gather_cores(pieces, gather_sides(pieces))

    residue_live = residue_mask.astype(f32)
    key_bias = jnp.broadcast_to(((residue_live - 1.0) * 1000000000.0)[:, None], (512, 128))
    cols_live = lax.dynamic_slice_in_dim(residue_live, head_index * 64, 64)
    rows_live = lax.dynamic_slice_in_dim(residue_live, row_index * 16, 16)
    row_live = alignment_row_mask.astype(f32)
    live = (row_live[:, None] * cols_live[None, :]).reshape(128, 1)
    mask_tile = jnp.zeros((8, 128), f32).at[0, 0:2].set(row_live)
    spots = jnp.asarray(SPOTS.reshape(-1))
    once = jnp.asarray(ONCE.reshape(-1))
    logits, values, gate = call(
        logits_kernel,
        vmem(7),
        vmem(3),
        [struct(2, 512, 512), struct(2, 2, 256, 512, dtype=bf16), struct(128, 256)],
        flops=3 * 2 * 1024 * 256 * 1024,
        touched=6 * MIB,
    )(
        everyone,
        sequence_matrix,
        attention_scale_vector[None],
        asking_factor_matrix,
        lookup_factor_matrix,
        content_factor_matrix,
        sigmoid_factor_matrix,
    )
    msa_out, left, right = call(
        attend_kernel,
        smem(1) + vmem(19),
        vmem(3),
        [struct(2, 64, 256), struct(4, 8, 128), struct(Z, 40, 128)],
        scratch=[pltpu.VMEM((32, 64, 128), f32), pltpu.VMEM((128, 128), f32)],
        flops=3 * 2 * 1024 * 512 * 256,
        touched=6 * MIB,
    )(
        spots,
        *bias,
        logits,
        key_bias,
        values,
        gate,
        sequence_matrix,
        final_factor_matrix,
        tensor_scale_vector[None],
        jnp.tile(first_factor_matrix, (1, 4)),
        second_factor_matrix.T,
        live,
        mask_tile,
    )
    planes = lax.all_to_all(
        right,
        "row",
        0,
        0,
        tiled=True,
        axis_index_groups=[[4 * z + a for z in range(Z)] for a in range(A)],
    )
    left = lax.ppermute(left, both, [(d, s) for s, d in moves(ONCE)])
    left, planes = after([left, planes])
    (spread,) = call(
        spread_kernel,
        vmem(1),
        hbm(1),
        [struct(A, H, 8, 128)],
        scratch=[pltpu.SemaphoreType.DMA((H,))],
    )(left)
    left = lax.all_to_all(
        spread.reshape(A * H, 8, 128),
        both,
        0,
        0,
        tiled=True,
        axis_index_groups=[[32 * z + k for k in range(32)] for z in range(Z)],
    )
    right = gather_cores([planes], after(gather_sides([planes]), left))
    (pair_out,) = call(
        outer_kernel,
        smem(2) + vmem(8),
        vmem(1),
        [struct(16, 64, 128)],
        scratch=[
            pltpu.VMEM((1280, 128), f32),
            pltpu.VMEM((256, 128), f32),
            pltpu.VMEM((512, 256), bf16),
            pltpu.VMEM((256, 2048), bf16),
        ],
        flops=3 * 2 * 1024 * 1024 * 256,
        touched=4 * MIB,
    )(
        once,
        rows_live,
        *right,
        left,
        outer_weight,
        pair_representation,
        cols_live[:, None],
    )
    return msa_out, pair_out


def solution(mesh):
    cells = P("row", "head", None)
    return jax.shard_map(
        body,
        mesh=mesh,
        in_specs=(cells, cells, P("row")) + (P(),) * 13,
        out_specs=(cells, cells),
        check_vma=False,
    )
```

```python
import itertools
import math

import jax
import jax.numpy as jnp
import numpy as np
from jax import lax
from jax.experimental import pallas as pl
from jax.experimental.pallas import tpu as pltpu
from jax.sharding import PartitionSpec as P

exact = lax.Precision.HIGHEST
f32 = jnp.float32
bf16 = jnp.bfloat16
MIB = 1024 * 1024

Z, A, H = 8, 4, 8
def ring(d, n):
    return min(d % n, -d % n)


def spread_tables():
    once = np.zeros((H, H), np.int32)
    twice = np.zeros((H, 2, H), np.int32)
    for c in range(H):
        hops = [
            [ring(h // 2 - c // 2, 4) + 2 * ((h ^ c) & 1) + ring(b - c, Z) for b in range(Z)]
            for h in range(H)
        ]
        flat = [hops[h][c] for h in range(H)]
        columns = sorted(range(H), key=lambda h: (-flat[h], h))
        planes = sorted(range(Z), key=lambda b: (ring(b - c, Z), (b - c) % Z))
        for h, b in zip(columns, planes):
            once[c][h] = b

        def fit(group, half):
            return min(
                (
                    (max(hops[h][b] for h, b in zip(group, p)), sum(hops[h][b] for h, b in zip(group, p)), p)
                    for p in itertools.permutations(range(4 * half, 4 * half + 4))
                )
            )

        best = None
        for low in itertools.combinations(range(H), 4):
            high = tuple(h for h in range(H) if h not in low)
            first = fit(low, 0), fit(high, 1)
            second = fit(low, 1), fit(high, 0)
            cost = (
                max(first[0][0], first[1][0]) + max(second[0][0], second[1][0]),
                sum(f[1] for f in first + second),
            )
            if best is None or cost < best[0]:
                best = cost, low, high, first, second
        _, low, high, first, second = best
        for k, fits in enumerate((first, second)):
            for group, found in zip((low, high), fits):
                for h, b in zip(group, found[2]):
                    twice[c][k][h] = b
    return once, twice


ONCE, TWICE = spread_tables()


def moves(table):
    return [
        ((4 * b + a) * H + h, (4 * int(table[b][h]) + a) * H + b)
        for b in range(Z)
        for a in range(A)
        for h in range(H)
    ]


def spots():
    out = np.zeros((H, 2, H), np.int32)
    for c in range(H):
        for k in range(2):
            for h in range(H):
                plane = int(TWICE[c][k][h])
                out[c][plane // 4][h] = 4 * k + plane % 4
    return out


SPOTS = spots()


def from_neighbour(v, bit):
    return lax.ppermute(v, "row", [(r, r ^ bit) for r in range(Z * A)])


def after(values, *others):
    return list(lax.optimization_barrier((*values, *others)))[: len(values)]


def gather_halves(first, second):
    own = jnp.concatenate([first, second], axis=0)
    near = jnp.concatenate([own, from_neighbour(own, 8)], axis=0)
    return [near, from_neighbour(near, 4)]


def gather_sides(pieces):
    return [from_neighbour(p, 2) for p in pieces]


def gather_cores(pieces, sides):
    return (
        pieces
        + [from_neighbour(p, 1) for p in pieces]
        + sides
        + [from_neighbour(p, 1) for p in sides]
    )


def side_of(row, source_side):
    return jnp.bitwise_xor(jnp.bitwise_and(row, 3), source_side) * 8


def half_position(row, spot, source_side):
    plane = jnp.bitwise_xor(jnp.bitwise_and(jnp.right_shift(row, 2), 3), jnp.bitwise_and(spot, 3))
    return (
        side_of(row, source_side)
        + jnp.bitwise_and(plane, 1) * 4
        + jnp.bitwise_and(plane, 2)
        + jnp.right_shift(spot, 2)
    )


def split(v):
    high = v.astype(bf16)
    return high, (v - high.astype(f32)).astype(bf16)


def dot(a, b, dims=((1,), (0,))):
    return lax.dot_general(a, b, (dims, ((), ())), preferred_element_type=f32)


def dot_exact(a, b, dims=((1,), (0,))):
    return lax.dot_general(a, b, (dims, ((), ())), precision=exact, preferred_element_type=f32)


def three(a, b, dims=((1,), (0,))):
    return dot(a[0], b[0], dims) + (dot(a[0], b[1], dims) + dot(a[1], b[0], dims))


def dot_three(a, b, dims=((1,), (0,))):
    return three(split(a), split(b), dims)


def norm_rows(v, gain):
    center = v - jnp.mean(v, axis=-1, keepdims=True)
    spread = jnp.mean(center * center, axis=-1, keepdims=True)
    return center * lax.rsqrt(spread + 1e-05) * gain


def start_all(copies):
    for copy in copies:
        copy.start()
    return copies


def wait_all(copies):
    for copy in copies:
        copy.wait()


def bias_kernel(
    pair_hbm,
    gain_hbm,
    weight_hbm,
    own_hbm,
    out_ref,
    copies_hbm,
    pair_ref,
    gain_ref,
    weight_ref,
    own_ref,
    sems,
):
    own_load = start_all([pltpu.make_async_copy(own_hbm, own_ref, sems.at[11])])
    loads = start_all(
        [
            pltpu.make_async_copy(gain_hbm, gain_ref, sems.at[8]),
            pltpu.make_async_copy(weight_hbm, weight_ref, sems.at[9]),
            pltpu.make_async_copy(pair_hbm, pair_ref, sems.at[10]),
        ]
    )
    wait_all(own_load)
    copies = start_all(
        [pltpu.make_async_copy(own_ref, copies_hbm.at[k], sems.at[k]) for k in range(H)]
    )
    wait_all(loads)
    rows = pair_ref[...].reshape(1024, 128)
    normed = norm_rows(rows, gain_ref[...])
    pick = lax.broadcasted_iota(jnp.int32, (8, 128), 0) == (
        lax.broadcasted_iota(jnp.int32, (8, 128), 1) // 16
    )
    wide = dot_exact(weight_ref[...], jnp.where(pick, 1.0, 0.0), ((0,), (0,)))
    result = dot_exact(normed, wide)
    lane = lax.broadcasted_iota(jnp.int32, (64, 128), 1) % 16
    total = jnp.zeros((64, 128), f32)
    for i in range(16):
        total = jnp.where(lane == i, result[64 * i : 64 * i + 64], total)
    out_ref[0] = total
    wait_all(copies)


def spread_kernel(left_ref, out_ref, sems):
    wait_all(
        start_all(
            [pltpu.make_async_copy(left_ref, out_ref.at[:, k], sems.at[k]) for k in range(H)]
        )
    )


def logits_kernel(
    all_ref, own_ref, gain_ref, wq_ref, wk_ref, wv_ref, wg_ref, logit_ref, value_ref, gate_ref
):
    gain = gain_ref[...]
    own = split(norm_rows(own_ref[...].reshape(128, 256), gain))
    query = three(own, split(wq_ref[...])) * (1.0 / math.sqrt(32))
    gate_ref[...] = jax.nn.sigmoid(three(own, split(wg_ref[...])))
    head_of_lane = lax.broadcasted_iota(jnp.int32, (128, 256), 1) // 32
    head_of_row = lax.broadcasted_iota(jnp.int32, (128, 256), 0) // 16
    keep = head_of_lane == head_of_row
    key_factor = split(wk_ref[...])
    value_factor = split(jnp.transpose(wv_ref[...]))
    for s in range(2):
        rows = split(
            norm_rows(jnp.concatenate([all_ref[b, s] for b in range(8)], axis=0), gain)
        )
        keys = split(three(rows, key_factor))
        value_ref[0, s], value_ref[1, s] = split(three(value_factor, rows, ((1,), (1,))))
        wide = []
        for a in range(4):
            part = query[64 * s + 16 * a : 64 * s + 16 * a + 16]
            wide.append(jnp.where(keep, jnp.concatenate([part] * 8, axis=0), 0.0))
        logit_ref[s] = three(keys, split(jnp.concatenate(wide, axis=0)), ((1,), (1,)))


def attend_kernel(
    spot_ref,
    *refs,
):
    attend(spot_ref, refs[:8], *refs[8:])


def attend(
    spot_ref,
    piece_refs,
    logit_ref,
    key_ref,
    value_ref,
    gate_ref,
    own_ref,
    wf_ref,
    gain_ref,
    first_ref,
    second_ref,
    live_ref,
    mask_ref,
    msa_ref,
    left_ref,
    right_ref,
    bias_ref,
    y_ref,
):
    for k, piece_ref in enumerate(piece_refs):
        bias_ref[4 * k : 4 * k + 4] = piece_ref[...]
    row = lax.axis_index("row")
    spots_at = (lax.axis_index("head") * 2 + jnp.right_shift(row, 4)) * H
    lane = lax.broadcasted_iota(jnp.int32, (32, 128), 1) // 16
    folded = [jnp.zeros((32, 128), f32) for _ in range(8)]
    for s in range(2):
        for pair in range(2):
            halves = []
            for a in (2 * pair, 2 * pair + 1):
                columns = pl.ds(128 * a, 128)
                tiles = []
                for b in range(8):
                    rows = pl.ds(64 * b, 64)
                    spot = half_position(row, spot_ref[spots_at + b], a)
                    tiles.append((logit_ref[s, rows, columns] + bias_ref[spot]) + key_ref[rows, :])
                logits = jnp.concatenate(tiles, axis=0)
                exponent = jnp.exp(logits - jnp.max(logits, axis=0, keepdims=True))
                weights = exponent * (1.0 / jnp.sum(exponent, axis=0, keepdims=True))
                halves.append(split(weights))
            part = three(
                (value_ref[0, s], value_ref[1, s]),
                [jnp.concatenate([halves[0][k], halves[1][k]], axis=1) for k in range(2)],
            )
            for e in range(2):
                a = 2 * pair + e
                for h in range(8):
                    moved = pltpu.roll(
                        part[32 * h : 32 * h + 32, 128 * e : 128 * e + 128],
                        (64 * s + 16 * a - 16 * h) % 128,
                        1,
                    )
                    folded[h] = jnp.where(lane == 4 * s + a, moved, folded[h])
    attended = jnp.transpose(jnp.concatenate(folded, axis=0)) * gate_ref[...]
    updated = own_ref[...].reshape(128, 256) + dot_three(attended, wf_ref[...])
    msa_ref[...] = updated.reshape(2, 64, 256)
    y = norm_rows(updated, gain_ref[...]) * live_ref[...]
    y = split(y)
    right = three(split(second_ref[...]), y, ((1,), (1,)))
    for k in range(Z):
        right_ref[k, 0:32, :] = right
        right_ref[k, 32:40, :] = mask_ref[...]
    y_ref[...] = three(y, split(first_ref[...]))
    lane = lax.broadcasted_iota(jnp.int32, (32, 128), 1) // 32
    left = jnp.zeros((32, 128), f32)
    for k in range(4):
        left = jnp.where(lane == k, y_ref[pl.ds(k, 32, stride=4), :], left)
    for s in range(2):
        for a in range(4):
            left_ref[a, 4 * s : 4 * s + 4, :] = left[16 * s + 4 * a : 16 * s + 4 * a + 4]


def outer_kernel(
    once_ref,
    rows_live_ref,
    *refs,
):
    outer_product(once_ref, rows_live_ref, refs[:4], *refs[4:])


def outer_product(
    once_ref,
    rows_live_ref,
    piece_refs,
    left_in_ref,
    weight_ref,
    pair_ref,
    cols_live_ref,
    out_ref,
    right_in_ref,
    sorted_ref,
    left_ref,
    right_ref,
    outer_ref,
):
    for q, piece_ref in enumerate(piece_refs):
        for k in range(Z):
            start = 40 * (Z * q + k)
            right_in_ref[start : start + 40, :] = piece_ref[k]
    row = lax.axis_index("row")
    for p in range(32):
        source = side_of(row, p // H) + once_ref[jnp.right_shift(row, 2) * H + p % H]
        spot = pl.multiple_of(source * 8, 8)
        sorted_ref[pl.ds(spot, 8), :] = left_in_ref[p]
    count = jnp.zeros((8, 128), f32)
    for k in range(32):
        count = count + right_in_ref[40 * k + 32 : 40 * k + 40, :]
    count = jnp.sum(count)
    left_rows = []
    for s in range(2):
        left_rows.append(
            jnp.concatenate(
                [sorted_ref[pl.ds(4 * s + q, 32, stride=8), :] for q in range(4)], axis=1
            )
        )
    left = jnp.concatenate(left_rows, axis=0)
    high = left.astype(bf16).astype(f32)
    low = left - high
    left_ref[...] = jnp.transpose(jnp.concatenate([high, high, low, jnp.zeros_like(low)], axis=0)).astype(bf16)
    lane = lax.broadcasted_iota(jnp.int32, (32, 128), 1) < 64
    for d in range(16):
        even = right_in_ref[pl.ds(2 * d, 32, stride=40), :]
        odd = right_in_ref[pl.ds(2 * d + 1, 32, stride=40), :]
        both = jnp.concatenate(
            [
                jnp.where(lane, even, pltpu.roll(odd, 64, 1)),
                jnp.where(lane, pltpu.roll(even, 64, 1), odd),
            ],
            axis=0,
        )
        high, low = split(both)
        columns = pl.ds(128 * d, 128)
        right_ref[0:64, columns] = high
        right_ref[64:128, columns] = low
        right_ref[128:192, columns] = high
        right_ref[192:256, columns] = jnp.zeros((64, 128), bf16)
    columns = [
        jnp.concatenate(
            [weight_ref[pl.ds(2 * d + e, 32, stride=32), :] for d in range(16)], axis=0
        )
        for e in range(2)
    ]
    weight = split(jnp.transpose(jnp.concatenate(columns, axis=1)))
    lane = lax.broadcasted_iota(jnp.int32, (128, 128), 1) < 64
    for n in range(8):
        columns = pl.ds(256 * n, 256)
        outer_ref[:, columns] = dot(left_ref[...], right_ref[:, columns])
    for q in range(8):
        stacked = jnp.concatenate(
            [
                jnp.concatenate(
                    [
                        outer_ref[64 * q + 32 * e : 64 * q + 32 * e + 32, 128 * d : 128 * d + 128]
                        for d in range(16)
                    ],
                    axis=0,
                )
                for e in range(2)
            ],
            axis=1,
        )
        y = three(weight, split(stacked))
        top, bottom = y[0:128], y[128:256]
        total = jnp.where(
            lane,
            top[:, 0:128] + pltpu.roll(bottom[:, 0:128], 64, 1),
            pltpu.roll(top[:, 128:256], 64, 1) + bottom[:, 128:256],
        )
        total = jnp.transpose(total)
        for e in range(2):
            i = 2 * q + e
            norm = count * rows_live_ref[i] * cols_live_ref[...] + 0.001
            out_ref[i] = pair_ref[i] + total[64 * e : 64 * e + 64] / norm


def vmem(count):
    return [pl.BlockSpec(memory_space=pltpu.VMEM)] * count


def smem(count):
    return [pl.BlockSpec(memory_space=pltpu.SMEM)] * count


def hbm(count):
    return [pl.BlockSpec(memory_space=pltpu.HBM)] * count


def struct(*shape, dtype=f32):
    return jax.ShapeDtypeStruct(shape, dtype)


def call(kernel, inputs, outputs, shapes, scratch=(), limit=32, flops=0, touched=0):
    return pl.pallas_call(
        kernel,
        in_specs=inputs,
        out_specs=outputs,
        out_shape=shapes,
        scratch_shapes=list(scratch),
        compiler_params=pltpu.CompilerParams(vmem_limit_bytes=limit * MIB),
        cost_estimate=pl.CostEstimate(flops=flops, bytes_accessed=touched, transcendentals=0),
    )


def body(
    sequence_matrix,
    pair_representation,
    alignment_row_mask,
    residue_mask,
    attention_scale_vector,
    asking_factor_matrix,
    lookup_factor_matrix,
    content_factor_matrix,
    sigmoid_factor_matrix,
    final_factor_matrix,
    pair_norm_gain,
    bias_weight,
    tensor_scale_vector,
    first_factor_matrix,
    second_factor_matrix,
    outer_weight,
):
    head_index = lax.axis_index("head")
    row_index = lax.axis_index("row")
    both = ("row", "head")
    block, copies = call(
        bias_kernel,
        hbm(4),
        vmem(1) + hbm(1),
        [struct(1, 64, 128), struct(H, 2, 64, 256)],
        scratch=[
            pltpu.VMEM((16, 64, 128), f32),
            pltpu.VMEM((1, 128), f32),
            pltpu.VMEM((8, 128), f32),
            pltpu.VMEM((2, 64, 256), f32),
            pltpu.SemaphoreType.DMA((H + 4,)),
        ],
        limit=60,
        flops=2 * 1024 * 128 * 128 * 6,
        touched=600000,
    )(pair_representation, pair_norm_gain[None], bias_weight.T, sequence_matrix)
    everyone = lax.all_to_all(copies, "head", 0, 0, tiled=True)
    pieces = gather_halves(
        lax.ppermute(block, both, moves(TWICE[:, 0])), lax.ppermute(block, both, moves(TWICE[:, 1]))
    )
    bias = gather_cores(pieces, gather_sides(pieces))

    residue_live = residue_mask.astype(f32)
    key_bias = jnp.broadcast_to(((residue_live - 1.0) * 1000000000.0)[:, None], (512, 128))
    cols_live = lax.dynamic_slice_in_dim(residue_live, head_index * 64, 64)
    rows_live = lax.dynamic_slice_in_dim(residue_live, row_index * 16, 16)
    row_live = alignment_row_mask.astype(f32)
    live = (row_live[:, None] * cols_live[None, :]).reshape(128, 1)
    mask_tile = jnp.zeros((8, 128), f32).at[0, 0:2].set(row_live)
    spots = jnp.asarray(SPOTS.reshape(-1))
    once = jnp.asarray(ONCE.reshape(-1))
    logits, values, gate = call(
        logits_kernel,
        vmem(7),
        vmem(3),
        [struct(2, 512, 512), struct(2, 2, 256, 512, dtype=bf16), struct(128, 256)],
        flops=3 * 2 * 1024 * 256 * 1024,
        touched=6 * MIB,
    )(
        everyone,
        sequence_matrix,
        attention_scale_vector[None],
        asking_factor_matrix,
        lookup_factor_matrix,
        content_factor_matrix,
        sigmoid_factor_matrix,
    )
    msa_out, left, right = call(
        attend_kernel,
        smem(1) + vmem(19),
        vmem(3),
        [struct(2, 64, 256), struct(4, 8, 128), struct(Z, 40, 128)],
        scratch=[pltpu.VMEM((32, 64, 128), f32), pltpu.VMEM((128, 128), f32)],
        flops=3 * 2 * 1024 * 512 * 256,
        touched=6 * MIB,
    )(
        spots,
        *bias,
        logits,
        key_bias,
        values,
        gate,
        sequence_matrix,
        final_factor_matrix,
        tensor_scale_vector[None],
        jnp.tile(first_factor_matrix, (1, 4)),
        second_factor_matrix.T,
        live,
        mask_tile,
    )
    planes = lax.all_to_all(
        right,
        "row",
        0,
        0,
        tiled=True,
        axis_index_groups=[[4 * z + a for z in range(Z)] for a in range(A)],
    )
    left = lax.ppermute(left, both, [(d, s) for s, d in moves(ONCE)])
    left, planes = after([left, planes])
    (spread,) = call(
        spread_kernel,
        vmem(1),
        hbm(1),
        [struct(A, H, 8, 128)],
        scratch=[pltpu.SemaphoreType.DMA((H,))],
    )(left)
    left = lax.all_to_all(
        spread.reshape(A * H, 8, 128),
        both,
        0,
        0,
        tiled=True,
        axis_index_groups=[[32 * z + k for k in range(32)] for z in range(Z)],
    )
    right = gather_cores([planes], after(gather_sides([planes]), left))
    (pair_out,) = call(
        outer_kernel,
        smem(2) + vmem(8),
        vmem(1),
        [struct(16, 64, 128)],
        scratch=[
            pltpu.VMEM((1280, 128), f32),
            pltpu.VMEM((256, 128), f32),
            pltpu.VMEM((512, 256), bf16),
            pltpu.VMEM((256, 2048), bf16),
            pltpu.VMEM((512, 2048), f32),
        ],
        flops=3 * 2 * 1024 * 1024 * 256,
        touched=4 * MIB,
    )(
        once,
        rows_live,
        *right,
        left,
        outer_weight,
        pair_representation,
        cols_live[:, None],
    )
    return msa_out, pair_out


def solution(mesh):
    cells = P("row", "head", None)
    return jax.shard_map(
        body,
        mesh=mesh,
        in_specs=(cells, cells, P("row")) + (P(),) * 13,
        out_specs=(cells, cells),
        check_vma=False,
    )
```

```python
import itertools
import math

import jax
import jax.numpy as jnp
import numpy as np
from jax import lax
from jax.experimental import pallas as pl
from jax.experimental.pallas import tpu as pltpu
from jax.sharding import PartitionSpec as P

exact = lax.Precision.HIGHEST
f32 = jnp.float32
bf16 = jnp.bfloat16
MIB = 1024 * 1024

Z, A, H = 8, 4, 8
def ring(d, n):
    return min(d % n, -d % n)


def spread_tables():
    once = np.zeros((H, H), np.int32)
    twice = np.zeros((H, 2, H), np.int32)
    for c in range(H):
        hops = [
            [ring(h // 2 - c // 2, 4) + 2 * ((h ^ c) & 1) + ring(b - c, Z) for b in range(Z)]
            for h in range(H)
        ]
        flat = [hops[h][c] for h in range(H)]
        columns = sorted(range(H), key=lambda h: (-flat[h], h))
        planes = sorted(range(Z), key=lambda b: (ring(b - c, Z), (b - c) % Z))
        for h, b in zip(columns, planes):
            once[c][h] = b

        def fit(group, half):
            return min(
                (
                    (max(hops[h][b] for h, b in zip(group, p)), sum(hops[h][b] for h, b in zip(group, p)), p)
                    for p in itertools.permutations(range(4 * half, 4 * half + 4))
                )
            )

        best = None
        for low in itertools.combinations(range(H), 4):
            high = tuple(h for h in range(H) if h not in low)
            first = fit(low, 0), fit(high, 1)
            second = fit(low, 1), fit(high, 0)
            cost = (
                max(first[0][0], first[1][0]) + max(second[0][0], second[1][0]),
                sum(f[1] for f in first + second),
            )
            if best is None or cost < best[0]:
                best = cost, low, high, first, second
        _, low, high, first, second = best
        if max(f[0] for f in first) < max(f[0] for f in second):
            first, second = second, first
        for k, fits in enumerate((first, second)):
            for group, found in zip((low, high), fits):
                for h, b in zip(group, found[2]):
                    twice[c][k][h] = b
    return once, twice


ONCE, TWICE = spread_tables()


def moves(table):
    return [
        ((4 * b + a) * H + h, (4 * int(table[b][h]) + a) * H + b)
        for b in range(Z)
        for a in range(A)
        for h in range(H)
    ]


def spots():
    out = np.zeros((H, 2, H), np.int32)
    for c in range(H):
        for k in range(2):
            for h in range(H):
                plane = int(TWICE[c][k][h])
                out[c][plane // 4][h] = 4 * k + plane % 4
    return out


SPOTS = spots()


def from_neighbour(v, bit):
    return lax.ppermute(v, "row", [(r, r ^ bit) for r in range(Z * A)])


def after(values, *others):
    return list(lax.optimization_barrier((*values, *others)))[: len(values)]


def gather_halves(first, second):
    own = jnp.concatenate([first, second], axis=0)
    near = jnp.concatenate([own, from_neighbour(own, 8)], axis=0)
    return [near, from_neighbour(near, 4)]


def gather_sides(pieces):
    return [from_neighbour(p, 2) for p in pieces]


def gather_cores(pieces, sides):
    return (
        pieces
        + [from_neighbour(p, 1) for p in pieces]
        + sides
        + [from_neighbour(p, 1) for p in sides]
    )


def side_of(row, source_side):
    return jnp.bitwise_xor(jnp.bitwise_and(row, 3), source_side) * 8


def half_position(row, spot, source_side):
    plane = jnp.bitwise_xor(jnp.bitwise_and(jnp.right_shift(row, 2), 3), jnp.bitwise_and(spot, 3))
    return (
        side_of(row, source_side)
        + jnp.bitwise_and(plane, 1) * 4
        + jnp.bitwise_and(plane, 2)
        + jnp.right_shift(spot, 2)
    )


def split(v):
    high = v.astype(bf16)
    return high, (v - high.astype(f32)).astype(bf16)


def dot(a, b, dims=((1,), (0,))):
    return lax.dot_general(a, b, (dims, ((), ())), preferred_element_type=f32)


def dot_exact(a, b, dims=((1,), (0,))):
    return lax.dot_general(a, b, (dims, ((), ())), precision=exact, preferred_element_type=f32)


def three(a, b, dims=((1,), (0,))):
    return dot(a[0], b[0], dims) + (dot(a[0], b[1], dims) + dot(a[1], b[0], dims))


def dot_three(a, b, dims=((1,), (0,))):
    return three(split(a), split(b), dims)


def norm_rows(v, gain):
    center = v - jnp.mean(v, axis=-1, keepdims=True)
    spread = jnp.mean(center * center, axis=-1, keepdims=True)
    return center * lax.rsqrt(spread + 1e-05) * gain


def start_all(copies):
    for copy in copies:
        copy.start()
    return copies


def wait_all(copies):
    for copy in copies:
        copy.wait()


def bias_kernel(
    pair_hbm,
    gain_hbm,
    weight_hbm,
    own_hbm,
    out_ref,
    copies_hbm,
    pair_ref,
    gain_ref,
    weight_ref,
    own_ref,
    sems,
):
    own_load = start_all([pltpu.make_async_copy(own_hbm, own_ref, sems.at[11])])
    loads = start_all(
        [
            pltpu.make_async_copy(gain_hbm, gain_ref, sems.at[8]),
            pltpu.make_async_copy(weight_hbm, weight_ref, sems.at[9]),
            pltpu.make_async_copy(pair_hbm, pair_ref, sems.at[10]),
        ]
    )
    wait_all(own_load)
    copies = start_all(
        [pltpu.make_async_copy(own_ref, copies_hbm.at[k], sems.at[k]) for k in range(H)]
    )
    wait_all(loads)
    rows = pair_ref[...].reshape(1024, 128)
    normed = norm_rows(rows, gain_ref[...])
    pick = lax.broadcasted_iota(jnp.int32, (8, 128), 0) == (
        lax.broadcasted_iota(jnp.int32, (8, 128), 1) // 16
    )
    wide = dot_exact(weight_ref[...], jnp.where(pick, 1.0, 0.0), ((0,), (0,)))
    result = dot_exact(normed, wide)
    lane = lax.broadcasted_iota(jnp.int32, (64, 128), 1) % 16
    total = jnp.zeros((64, 128), f32)
    for i in range(16):
        total = jnp.where(lane == i, result[64 * i : 64 * i + 64], total)
    out_ref[0] = total
    wait_all(copies)


def spread_kernel(left_ref, out_ref, sems):
    wait_all(
        start_all(
            [pltpu.make_async_copy(left_ref, out_ref.at[:, k], sems.at[k]) for k in range(H)]
        )
    )


def logits_kernel(
    all_ref, own_ref, gain_ref, wq_ref, wk_ref, wv_ref, wg_ref, logit_ref, value_ref, gate_ref
):
    gain = gain_ref[...]
    own = split(norm_rows(own_ref[...].reshape(128, 256), gain))
    query = three(own, split(wq_ref[...])) * (1.0 / math.sqrt(32))
    gate_ref[...] = jax.nn.sigmoid(three(own, split(wg_ref[...])))
    head_of_lane = lax.broadcasted_iota(jnp.int32, (128, 256), 1) // 32
    head_of_row = lax.broadcasted_iota(jnp.int32, (128, 256), 0) // 16
    keep = head_of_lane == head_of_row
    key_factor = split(wk_ref[...])
    value_factor = split(jnp.transpose(wv_ref[...]))
    for s in range(2):
        rows = split(
            norm_rows(jnp.concatenate([all_ref[b, s] for b in range(8)], axis=0), gain)
        )
        keys = split(three(rows, key_factor))
        value_ref[0, s], value_ref[1, s] = split(three(value_factor, rows, ((1,), (1,))))
        wide = []
        for a in range(4):
            part = query[64 * s + 16 * a : 64 * s + 16 * a + 16]
            wide.append(jnp.where(keep, jnp.concatenate([part] * 8, axis=0), 0.0))
        logit_ref[s] = three(keys, split(jnp.concatenate(wide, axis=0)), ((1,), (1,)))


def attend_kernel(
    spot_ref,
    *refs,
):
    attend(spot_ref, refs[:8], *refs[8:])


def attend(
    spot_ref,
    piece_refs,
    logit_ref,
    key_ref,
    value_ref,
    gate_ref,
    own_ref,
    wf_ref,
    gain_ref,
    first_ref,
    second_ref,
    live_ref,
    mask_ref,
    msa_ref,
    left_ref,
    right_ref,
    bias_ref,
    y_ref,
):
    for k, piece_ref in enumerate(piece_refs):
        bias_ref[4 * k : 4 * k + 4] = piece_ref[...]
    row = lax.axis_index("row")
    spots_at = (lax.axis_index("head") * 2 + jnp.right_shift(row, 4)) * H
    lane = lax.broadcasted_iota(jnp.int32, (32, 128), 1) // 16
    folded = [jnp.zeros((32, 128), f32) for _ in range(8)]
    for s in range(2):
        for pair in range(2):
            halves = []
            for a in (2 * pair, 2 * pair + 1):
                columns = pl.ds(128 * a, 128)
                tiles = []
                for b in range(8):
                    rows = pl.ds(64 * b, 64)
                    spot = half_position(row, spot_ref[spots_at + b], a)
                    tiles.append((logit_ref[s, rows, columns] + bias_ref[spot]) + key_ref[rows, :])
                logits = jnp.concatenate(tiles, axis=0)
                exponent = jnp.exp(logits - jnp.max(logits, axis=0, keepdims=True))
                weights = exponent * (1.0 / jnp.sum(exponent, axis=0, keepdims=True))
                halves.append(split(weights))
            part = three(
                (value_ref[0, s], value_ref[1, s]),
                [jnp.concatenate([halves[0][k], halves[1][k]], axis=1) for k in range(2)],
            )
            for e in range(2):
                a = 2 * pair + e
                for h in range(8):
                    moved = pltpu.roll(
                        part[32 * h : 32 * h + 32, 128 * e : 128 * e + 128],
                        (64 * s + 16 * a - 16 * h) % 128,
                        1,
                    )
                    folded[h] = jnp.where(lane == 4 * s + a, moved, folded[h])
    attended = jnp.transpose(jnp.concatenate(folded, axis=0)) * gate_ref[...]
    updated = own_ref[...].reshape(128, 256) + dot_three(attended, wf_ref[...])
    msa_ref[...] = updated.reshape(2, 64, 256)
    y = norm_rows(updated, gain_ref[...]) * live_ref[...]
    y = split(y)
    right = three(split(second_ref[...]), y, ((1,), (1,)))
    for k in range(Z):
        right_ref[k, 0:32, :] = right
        right_ref[k, 32:40, :] = mask_ref[...]
    y_ref[...] = three(y, split(first_ref[...]))
    lane = lax.broadcasted_iota(jnp.int32, (32, 128), 1) // 32
    left = jnp.zeros((32, 128), f32)
    for k in range(4):
        left = jnp.where(lane == k, y_ref[pl.ds(k, 32, stride=4), :], left)
    for s in range(2):
        for a in range(4):
            left_ref[a, 4 * s : 4 * s + 4, :] = left[16 * s + 4 * a : 16 * s + 4 * a + 4]


def outer_kernel(
    once_ref,
    rows_live_ref,
    *refs,
):
    outer_product(once_ref, rows_live_ref, refs[:4], *refs[4:])


def outer_product(
    once_ref,
    rows_live_ref,
    piece_refs,
    left_in_ref,
    weight_ref,
    pair_ref,
    cols_live_ref,
    out_ref,
    right_in_ref,
    sorted_ref,
    left_ref,
    right_ref,
    outer_ref,
):
    for q, piece_ref in enumerate(piece_refs):
        for k in range(Z):
            start = 40 * (Z * q + k)
            right_in_ref[start : start + 40, :] = piece_ref[k]
    row = lax.axis_index("row")
    for p in range(32):
        source = side_of(row, p // H) + once_ref[jnp.right_shift(row, 2) * H + p % H]
        spot = pl.multiple_of(source * 8, 8)
        sorted_ref[pl.ds(spot, 8), :] = left_in_ref[p]
    count = jnp.zeros((8, 128), f32)
    for k in range(32):
        count = count + right_in_ref[40 * k + 32 : 40 * k + 40, :]
    count = jnp.sum(count)
    left_rows = []
    for s in range(2):
        left_rows.append(
            jnp.concatenate(
                [sorted_ref[pl.ds(4 * s + q, 32, stride=8), :] for q in range(4)], axis=1
            )
        )
    left = jnp.concatenate(left_rows, axis=0)
    high = left.astype(bf16).astype(f32)
    halves = jnp.transpose(jnp.concatenate([high, left - high], axis=0))
    lane = lax.broadcasted_iota(jnp.int32, (512, 128), 1) < 64
    left_ref[:, 0:128] = halves.astype(bf16)
    left_ref[:, 128:256] = jnp.where(lane, halves, 0.0).astype(bf16)
    lane = lax.broadcasted_iota(jnp.int32, (32, 128), 1) < 64
    for d in range(16):
        even = right_in_ref[pl.ds(2 * d, 32, stride=40), :]
        odd = right_in_ref[pl.ds(2 * d + 1, 32, stride=40), :]
        both = jnp.concatenate(
            [
                jnp.where(lane, even, pltpu.roll(odd, 64, 1)),
                jnp.where(lane, pltpu.roll(even, 64, 1), odd),
            ],
            axis=0,
        )
        high, low = split(both)
        columns = pl.ds(128 * d, 128)
        right_ref[0:64, columns] = high
        right_ref[64:128, columns] = high
        right_ref[128:192, columns] = low
        right_ref[192:256, columns] = jnp.zeros((64, 128), bf16)
    columns = [
        jnp.concatenate(
            [weight_ref[pl.ds(2 * d + e, 32, stride=32), :] for d in range(16)], axis=0
        )
        for e in range(2)
    ]
    weight = split(jnp.transpose(jnp.concatenate(columns, axis=1)))
    lane = lax.broadcasted_iota(jnp.int32, (128, 128), 1) < 64
    for n in range(8):
        columns = pl.ds(256 * n, 256)
        outer_ref[:, columns] = dot(left_ref[...], right_ref[:, columns])
    for q in range(8):
        stacked = jnp.concatenate(
            [
                jnp.concatenate(
                    [
                        outer_ref[64 * q + 32 * e : 64 * q + 32 * e + 32, 128 * d : 128 * d + 128]
                        for d in range(16)
                    ],
                    axis=0,
                )
                for e in range(2)
            ],
            axis=1,
        )
        y = three(weight, split(stacked))
        top, bottom = y[0:128], y[128:256]
        total = jnp.where(
            lane,
            top[:, 0:128] + pltpu.roll(bottom[:, 0:128], 64, 1),
            pltpu.roll(top[:, 128:256], 64, 1) + bottom[:, 128:256],
        )
        total = jnp.transpose(total)
        for e in range(2):
            i = 2 * q + e
            norm = count * rows_live_ref[i] * cols_live_ref[...] + 0.001
            out_ref[i] = pair_ref[i] + total[64 * e : 64 * e + 64] / norm


def vmem(count):
    return [pl.BlockSpec(memory_space=pltpu.VMEM)] * count


def smem(count):
    return [pl.BlockSpec(memory_space=pltpu.SMEM)] * count


def hbm(count):
    return [pl.BlockSpec(memory_space=pltpu.HBM)] * count


def struct(*shape, dtype=f32):
    return jax.ShapeDtypeStruct(shape, dtype)


def call(kernel, inputs, outputs, shapes, scratch=(), limit=32, flops=0, touched=0):
    return pl.pallas_call(
        kernel,
        in_specs=inputs,
        out_specs=outputs,
        out_shape=shapes,
        scratch_shapes=list(scratch),
        compiler_params=pltpu.CompilerParams(vmem_limit_bytes=limit * MIB),
        cost_estimate=pl.CostEstimate(flops=flops, bytes_accessed=touched, transcendentals=0),
    )


def body(
    sequence_matrix,
    pair_representation,
    alignment_row_mask,
    residue_mask,
    attention_scale_vector,
    asking_factor_matrix,
    lookup_factor_matrix,
    content_factor_matrix,
    sigmoid_factor_matrix,
    final_factor_matrix,
    pair_norm_gain,
    bias_weight,
    tensor_scale_vector,
    first_factor_matrix,
    second_factor_matrix,
    outer_weight,
):
    head_index = lax.axis_index("head")
    row_index = lax.axis_index("row")
    both = ("row", "head")
    block, copies = call(
        bias_kernel,
        hbm(4),
        vmem(1) + hbm(1),
        [struct(1, 64, 128), struct(H, 2, 64, 256)],
        scratch=[
            pltpu.VMEM((16, 64, 128), f32),
            pltpu.VMEM((1, 128), f32),
            pltpu.VMEM((8, 128), f32),
            pltpu.VMEM((2, 64, 256), f32),
            pltpu.SemaphoreType.DMA((H + 4,)),
        ],
        limit=60,
        flops=2 * 1024 * 128 * 128 * 6,
        touched=600000,
    )(pair_representation, pair_norm_gain[None], bias_weight.T, sequence_matrix)
    everyone = lax.all_to_all(copies, "head", 0, 0, tiled=True)
    pieces = gather_halves(
        lax.ppermute(block, both, moves(TWICE[:, 0])), lax.ppermute(block, both, moves(TWICE[:, 1]))
    )
    bias = gather_cores(pieces, gather_sides(pieces))

    residue_live = residue_mask.astype(f32)
    key_bias = jnp.broadcast_to(((residue_live - 1.0) * 1000000000.0)[:, None], (512, 128))
    cols_live = lax.dynamic_slice_in_dim(residue_live, head_index * 64, 64)
    rows_live = lax.dynamic_slice_in_dim(residue_live, row_index * 16, 16)
    row_live = alignment_row_mask.astype(f32)
    live = (row_live[:, None] * cols_live[None, :]).reshape(128, 1)
    mask_tile = jnp.zeros((8, 128), f32).at[0, 0:2].set(row_live)
    spots = jnp.asarray(SPOTS.reshape(-1))
    once = jnp.asarray(ONCE.reshape(-1))
    logits, values, gate = call(
        logits_kernel,
        vmem(7),
        vmem(3),
        [struct(2, 512, 512), struct(2, 2, 256, 512, dtype=bf16), struct(128, 256)],
        flops=3 * 2 * 1024 * 256 * 1024,
        touched=6 * MIB,
    )(
        everyone,
        sequence_matrix,
        attention_scale_vector[None],
        asking_factor_matrix,
        lookup_factor_matrix,
        content_factor_matrix,
        sigmoid_factor_matrix,
    )
    msa_out, left, right = call(
        attend_kernel,
        smem(1) + vmem(19),
        vmem(3),
        [struct(2, 64, 256), struct(4, 8, 128), struct(Z, 40, 128)],
        scratch=[pltpu.VMEM((32, 64, 128), f32), pltpu.VMEM((128, 128), f32)],
        flops=3 * 2 * 1024 * 512 * 256,
        touched=6 * MIB,
    )(
        spots,
        *bias,
        logits,
        key_bias,
        values,
        gate,
        sequence_matrix,
        final_factor_matrix,
        tensor_scale_vector[None],
        jnp.tile(first_factor_matrix, (1, 4)),
        second_factor_matrix.T,
        live,
        mask_tile,
    )
    planes = lax.all_to_all(
        right,
        "row",
        0,
        0,
        tiled=True,
        axis_index_groups=[[4 * z + a for z in range(Z)] for a in range(A)],
    )
    left = lax.ppermute(left, both, [(d, s) for s, d in moves(ONCE)])
    left, planes = after([left, planes])
    (spread,) = call(
        spread_kernel,
        vmem(1),
        hbm(1),
        [struct(A, H, 8, 128)],
        scratch=[pltpu.SemaphoreType.DMA((H,))],
    )(left)
    left = lax.all_to_all(
        spread.reshape(A * H, 8, 128),
        both,
        0,
        0,
        tiled=True,
        axis_index_groups=[[32 * z + k for k in range(32)] for z in range(Z)],
    )
    right = gather_cores([planes], after(gather_sides([planes]), left))
    (pair_out,) = call(
        outer_kernel,
        smem(2) + vmem(8),
        vmem(1),
        [struct(16, 64, 128)],
        scratch=[
            pltpu.VMEM((1280, 128), f32),
            pltpu.VMEM((256, 128), f32),
            pltpu.VMEM((512, 256), bf16),
            pltpu.VMEM((256, 2048), bf16),
            pltpu.VMEM((512, 2048), f32),
        ],
        flops=3 * 2 * 1024 * 1024 * 256,
        touched=4 * MIB,
    )(
        once,
        rows_live,
        *right,
        left,
        outer_weight,
        pair_representation,
        cols_live[:, None],
    )
    return msa_out, pair_out


def solution(mesh):
    cells = P("row", "head", None)
    return jax.shard_map(
        body,
        mesh=mesh,
        in_specs=(cells, cells, P("row")) + (P(),) * 13,
        out_specs=(cells, cells),
        check_vma=False,
    )
```

```python
import itertools
import math

import jax
import jax.numpy as jnp
import numpy as np
from jax import lax
from jax.experimental import pallas as pl
from jax.experimental.pallas import tpu as pltpu
from jax.sharding import PartitionSpec as P

exact = lax.Precision.HIGHEST
f32 = jnp.float32
bf16 = jnp.bfloat16
MIB = 1024 * 1024

Z, A, H = 8, 4, 8
def ring(d, n):
    return min(d % n, -d % n)


def spread_tables():
    once = np.zeros((H, H), np.int32)
    twice = np.zeros((H, 2, H), np.int32)
    for c in range(H):
        hops = [
            [ring(h // 2 - c // 2, 4) + 2 * ((h ^ c) & 1) + ring(b - c, Z) for b in range(Z)]
            for h in range(H)
        ]
        flat = [hops[h][c] for h in range(H)]
        columns = sorted(range(H), key=lambda h: (-flat[h], (h // 2 - c // 2) % 4))
        planes = sorted(range(Z), key=lambda b: (ring(b - c, Z), (b - c) % Z))
        for h, b in zip(columns, planes):
            once[c][h] = b

        def fit(group, half):
            return min(
                (
                    (max(hops[h][b] for h, b in zip(group, p)), sum(hops[h][b] for h, b in zip(group, p)), p)
                    for p in itertools.permutations(range(4 * half, 4 * half + 4))
                )
            )

        best = None
        for low in itertools.combinations(range(H), 4):
            high = tuple(h for h in range(H) if h not in low)
            first = fit(low, 0), fit(high, 1)
            second = fit(low, 1), fit(high, 0)
            cost = (
                max(first[0][0], first[1][0]) + max(second[0][0], second[1][0]),
                sum(f[1] for f in first + second),
            )
            if best is None or cost < best[0]:
                best = cost, low, high, first, second
        _, low, high, first, second = best
        if max(f[0] for f in first) < max(f[0] for f in second):
            first, second = second, first
        for k, fits in enumerate((first, second)):
            for group, found in zip((low, high), fits):
                for h, b in zip(group, found[2]):
                    twice[c][k][h] = b
    return once, twice


ONCE, TWICE = spread_tables()


def moves(table):
    return [
        ((4 * b + a) * H + h, (4 * int(table[b][h]) + a) * H + b)
        for b in range(Z)
        for a in range(A)
        for h in range(H)
    ]


def spots():
    out = np.zeros((H, 2, H), np.int32)
    for c in range(H):
        for k in range(2):
            for h in range(H):
                plane = int(TWICE[c][k][h])
                out[c][plane // 4][h] = 4 * k + plane % 4
    return out


SPOTS = spots()


def from_neighbour(v, bit):
    return lax.ppermute(v, "row", [(r, r ^ bit) for r in range(Z * A)])


def after(values, *others):
    return list(lax.optimization_barrier((*values, *others)))[: len(values)]


def gather_halves(first, second):
    own = jnp.concatenate([first, second], axis=0)
    near = jnp.concatenate([own, from_neighbour(own, 8)], axis=0)
    return [near, from_neighbour(near, 4)]


def gather_sides(pieces):
    return [from_neighbour(p, 2) for p in pieces]


def gather_cores(pieces, sides):
    return (
        pieces
        + [from_neighbour(p, 1) for p in pieces]
        + sides
        + [from_neighbour(p, 1) for p in sides]
    )


def side_of(row, source_side):
    return jnp.bitwise_xor(jnp.bitwise_and(row, 3), source_side) * 8


def half_position(row, spot, source_side):
    plane = jnp.bitwise_xor(jnp.bitwise_and(jnp.right_shift(row, 2), 3), jnp.bitwise_and(spot, 3))
    return (
        side_of(row, source_side)
        + jnp.bitwise_and(plane, 1) * 4
        + jnp.bitwise_and(plane, 2)
        + jnp.right_shift(spot, 2)
    )


def split(v):
    high = v.astype(bf16)
    return high, (v - high.astype(f32)).astype(bf16)


def dot(a, b, dims=((1,), (0,))):
    return lax.dot_general(a, b, (dims, ((), ())), preferred_element_type=f32)


def dot_exact(a, b, dims=((1,), (0,))):
    return lax.dot_general(a, b, (dims, ((), ())), precision=exact, preferred_element_type=f32)


def three(a, b, dims=((1,), (0,))):
    return dot(a[0], b[0], dims) + (dot(a[0], b[1], dims) + dot(a[1], b[0], dims))


def dot_three(a, b, dims=((1,), (0,))):
    return three(split(a), split(b), dims)


def norm_rows(v, gain):
    center = v - jnp.mean(v, axis=-1, keepdims=True)
    spread = jnp.mean(center * center, axis=-1, keepdims=True)
    return center * lax.rsqrt(spread + 1e-05) * gain


def start_all(copies):
    for copy in copies:
        copy.start()
    return copies


def wait_all(copies):
    for copy in copies:
        copy.wait()


def bias_kernel(
    pair_hbm,
    gain_hbm,
    weight_hbm,
    own_hbm,
    out_ref,
    copies_hbm,
    pair_ref,
    gain_ref,
    weight_ref,
    own_ref,
    sems,
):
    own_load = start_all([pltpu.make_async_copy(own_hbm, own_ref, sems.at[11])])
    loads = start_all(
        [
            pltpu.make_async_copy(gain_hbm, gain_ref, sems.at[8]),
            pltpu.make_async_copy(weight_hbm, weight_ref, sems.at[9]),
            pltpu.make_async_copy(pair_hbm, pair_ref, sems.at[10]),
        ]
    )
    wait_all(own_load)
    copies = start_all(
        [pltpu.make_async_copy(own_ref, copies_hbm.at[k], sems.at[k]) for k in range(H)]
    )
    wait_all(loads)
    rows = pair_ref[...].reshape(1024, 128)
    normed = norm_rows(rows, gain_ref[...])
    pick = lax.broadcasted_iota(jnp.int32, (8, 128), 0) == (
        lax.broadcasted_iota(jnp.int32, (8, 128), 1) // 16
    )
    wide = dot_exact(weight_ref[...], jnp.where(pick, 1.0, 0.0), ((0,), (0,)))
    result = dot_exact(normed, wide)
    lane = lax.broadcasted_iota(jnp.int32, (64, 128), 1) % 16
    total = jnp.zeros((64, 128), f32)
    for i in range(16):
        total = jnp.where(lane == i, result[64 * i : 64 * i + 64], total)
    out_ref[0] = total
    wait_all(copies)


def spread_kernel(left_ref, out_ref, sems):
    wait_all(
        start_all(
            [pltpu.make_async_copy(left_ref, out_ref.at[:, k], sems.at[k]) for k in range(H)]
        )
    )


def logits_kernel(
    all_ref, own_ref, gain_ref, wq_ref, wk_ref, wv_ref, wg_ref, logit_ref, value_ref, gate_ref
):
    gain = gain_ref[...]
    own = split(norm_rows(own_ref[...].reshape(128, 256), gain))
    query = three(own, split(wq_ref[...])) * (1.0 / math.sqrt(32))
    gate_ref[...] = jax.nn.sigmoid(three(own, split(wg_ref[...])))
    head_of_lane = lax.broadcasted_iota(jnp.int32, (128, 256), 1) // 32
    head_of_row = lax.broadcasted_iota(jnp.int32, (128, 256), 0) // 16
    keep = head_of_lane == head_of_row
    key_factor = split(wk_ref[...])
    value_factor = split(jnp.transpose(wv_ref[...]))
    for s in range(2):
        rows = split(
            norm_rows(jnp.concatenate([all_ref[b, s] for b in range(8)], axis=0), gain)
        )
        keys = split(three(rows, key_factor))
        value_ref[0, s], value_ref[1, s] = split(three(value_factor, rows, ((1,), (1,))))
        wide = []
        for a in range(4):
            part = query[64 * s + 16 * a : 64 * s + 16 * a + 16]
            wide.append(jnp.where(keep, jnp.concatenate([part] * 8, axis=0), 0.0))
        logit_ref[s] = three(keys, split(jnp.concatenate(wide, axis=0)), ((1,), (1,)))


def attend_kernel(
    spot_ref,
    *refs,
):
    attend(spot_ref, refs[:8], *refs[8:])


def attend(
    spot_ref,
    piece_refs,
    logit_ref,
    key_ref,
    value_ref,
    gate_ref,
    own_ref,
    wf_ref,
    gain_ref,
    first_ref,
    second_ref,
    live_ref,
    mask_ref,
    msa_ref,
    left_ref,
    right_ref,
    bias_ref,
    y_ref,
):
    for k, piece_ref in enumerate(piece_refs):
        bias_ref[4 * k : 4 * k + 4] = piece_ref[...]
    row = lax.axis_index("row")
    spots_at = (lax.axis_index("head") * 2 + jnp.right_shift(row, 4)) * H
    lane = lax.broadcasted_iota(jnp.int32, (32, 128), 1) // 16
    folded = [jnp.zeros((32, 128), f32) for _ in range(8)]
    for s in range(2):
        for pair in range(2):
            halves = []
            for a in (2 * pair, 2 * pair + 1):
                columns = pl.ds(128 * a, 128)
                tiles = []
                for b in range(8):
                    rows = pl.ds(64 * b, 64)
                    spot = half_position(row, spot_ref[spots_at + b], a)
                    tiles.append((logit_ref[s, rows, columns] + bias_ref[spot]) + key_ref[rows, :])
                logits = jnp.concatenate(tiles, axis=0)
                exponent = jnp.exp(logits - jnp.max(logits, axis=0, keepdims=True))
                weights = exponent * (1.0 / jnp.sum(exponent, axis=0, keepdims=True))
                halves.append(split(weights))
            part = three(
                (value_ref[0, s], value_ref[1, s]),
                [jnp.concatenate([halves[0][k], halves[1][k]], axis=1) for k in range(2)],
            )
            for e in range(2):
                a = 2 * pair + e
                for h in range(8):
                    moved = pltpu.roll(
                        part[32 * h : 32 * h + 32, 128 * e : 128 * e + 128],
                        (64 * s + 16 * a - 16 * h) % 128,
                        1,
                    )
                    folded[h] = jnp.where(lane == 4 * s + a, moved, folded[h])
    attended = jnp.transpose(jnp.concatenate(folded, axis=0)) * gate_ref[...]
    updated = own_ref[...].reshape(128, 256) + dot_three(attended, wf_ref[...])
    msa_ref[...] = updated.reshape(2, 64, 256)
    y = norm_rows(updated, gain_ref[...]) * live_ref[...]
    y = split(y)
    right = three(split(second_ref[...]), y, ((1,), (1,)))
    for k in range(Z):
        right_ref[k, 0:32, :] = right
        right_ref[k, 32:40, :] = mask_ref[...]
    y_ref[...] = three(y, split(first_ref[...]))
    lane = lax.broadcasted_iota(jnp.int32, (32, 128), 1) // 32
    left = jnp.zeros((32, 128), f32)
    for k in range(4):
        left = jnp.where(lane == k, y_ref[pl.ds(k, 32, stride=4), :], left)
    for s in range(2):
        for a in range(4):
            left_ref[a, 4 * s : 4 * s + 4, :] = left[16 * s + 4 * a : 16 * s + 4 * a + 4]


def outer_kernel(
    once_ref,
    rows_live_ref,
    *refs,
):
    outer_product(once_ref, rows_live_ref, refs[:4], *refs[4:])


def outer_product(
    once_ref,
    rows_live_ref,
    piece_refs,
    left_in_ref,
    weight_ref,
    pair_ref,
    cols_live_ref,
    out_ref,
    right_in_ref,
    sorted_ref,
    left_ref,
    right_ref,
    outer_ref,
):
    for q, piece_ref in enumerate(piece_refs):
        for k in range(Z):
            start = 40 * (Z * q + k)
            right_in_ref[start : start + 40, :] = piece_ref[k]
    row = lax.axis_index("row")
    for p in range(32):
        source = side_of(row, p // H) + once_ref[jnp.right_shift(row, 2) * H + p % H]
        spot = pl.multiple_of(source * 8, 8)
        sorted_ref[pl.ds(spot, 8), :] = left_in_ref[p]
    count = jnp.zeros((8, 128), f32)
    for k in range(32):
        count = count + right_in_ref[40 * k + 32 : 40 * k + 40, :]
    count = jnp.sum(count)
    left_rows = []
    for s in range(2):
        left_rows.append(
            jnp.concatenate(
                [sorted_ref[pl.ds(4 * s + q, 32, stride=8), :] for q in range(4)], axis=1
            )
        )
    left = jnp.concatenate(left_rows, axis=0)
    high = left.astype(bf16).astype(f32)
    halves = jnp.transpose(jnp.concatenate([high, left - high], axis=0))
    lane = lax.broadcasted_iota(jnp.int32, (512, 128), 1) < 64
    left_ref[:, 0:128] = halves.astype(bf16)
    left_ref[:, 128:256] = jnp.where(lane, halves, 0.0).astype(bf16)
    lane = lax.broadcasted_iota(jnp.int32, (32, 128), 1) < 64
    for d in range(16):
        even = right_in_ref[pl.ds(2 * d, 32, stride=40), :]
        odd = right_in_ref[pl.ds(2 * d + 1, 32, stride=40), :]
        both = jnp.concatenate(
            [
                jnp.where(lane, even, pltpu.roll(odd, 64, 1)),
                jnp.where(lane, pltpu.roll(even, 64, 1), odd),
            ],
            axis=0,
        )
        high, low = split(both)
        columns = pl.ds(128 * d, 128)
        right_ref[0:64, columns] = high
        right_ref[64:128, columns] = high
        right_ref[128:192, columns] = low
        right_ref[192:256, columns] = jnp.zeros((64, 128), bf16)
    columns = [
        jnp.concatenate(
            [weight_ref[pl.ds(2 * d + e, 32, stride=32), :] for d in range(16)], axis=0
        )
        for e in range(2)
    ]
    weight = split(jnp.transpose(jnp.concatenate(columns, axis=1)))
    lane = lax.broadcasted_iota(jnp.int32, (128, 128), 1) < 64
    for n in range(8):
        columns = pl.ds(256 * n, 256)
        outer_ref[:, columns] = dot(left_ref[...], right_ref[:, columns])
    for q in range(8):
        stacked = jnp.concatenate(
            [
                jnp.concatenate(
                    [
                        outer_ref[64 * q + 32 * e : 64 * q + 32 * e + 32, 128 * d : 128 * d + 128]
                        for d in range(16)
                    ],
                    axis=0,
                )
                for e in range(2)
            ],
            axis=1,
        )
        y = three(weight, split(stacked))
        top, bottom = y[0:128], y[128:256]
        total = jnp.where(
            lane,
            top[:, 0:128] + pltpu.roll(bottom[:, 0:128], 64, 1),
            pltpu.roll(top[:, 128:256], 64, 1) + bottom[:, 128:256],
        )
        total = jnp.transpose(total)
        for e in range(2):
            i = 2 * q + e
            norm = count * rows_live_ref[i] * cols_live_ref[...] + 0.001
            out_ref[i] = pair_ref[i] + total[64 * e : 64 * e + 64] / norm


def vmem(count):
    return [pl.BlockSpec(memory_space=pltpu.VMEM)] * count


def smem(count):
    return [pl.BlockSpec(memory_space=pltpu.SMEM)] * count


def hbm(count):
    return [pl.BlockSpec(memory_space=pltpu.HBM)] * count


def struct(*shape, dtype=f32):
    return jax.ShapeDtypeStruct(shape, dtype)


def call(kernel, inputs, outputs, shapes, scratch=(), limit=32, flops=0, touched=0):
    return pl.pallas_call(
        kernel,
        in_specs=inputs,
        out_specs=outputs,
        out_shape=shapes,
        scratch_shapes=list(scratch),
        compiler_params=pltpu.CompilerParams(vmem_limit_bytes=limit * MIB),
        cost_estimate=pl.CostEstimate(flops=flops, bytes_accessed=touched, transcendentals=0),
    )


def body(
    sequence_matrix,
    pair_representation,
    alignment_row_mask,
    residue_mask,
    attention_scale_vector,
    asking_factor_matrix,
    lookup_factor_matrix,
    content_factor_matrix,
    sigmoid_factor_matrix,
    final_factor_matrix,
    pair_norm_gain,
    bias_weight,
    tensor_scale_vector,
    first_factor_matrix,
    second_factor_matrix,
    outer_weight,
):
    head_index = lax.axis_index("head")
    row_index = lax.axis_index("row")
    both = ("row", "head")
    block, copies = call(
        bias_kernel,
        hbm(4),
        vmem(1) + hbm(1),
        [struct(1, 64, 128), struct(H, 2, 64, 256)],
        scratch=[
            pltpu.VMEM((16, 64, 128), f32),
            pltpu.VMEM((1, 128), f32),
            pltpu.VMEM((8, 128), f32),
            pltpu.VMEM((2, 64, 256), f32),
            pltpu.SemaphoreType.DMA((H + 4,)),
        ],
        limit=60,
        flops=2 * 1024 * 128 * 128 * 6,
        touched=600000,
    )(pair_representation, pair_norm_gain[None], bias_weight.T, sequence_matrix)
    everyone = lax.all_to_all(copies, "head", 0, 0, tiled=True)
    pieces = gather_halves(
        lax.ppermute(block, both, moves(TWICE[:, 0])), lax.ppermute(block, both, moves(TWICE[:, 1]))
    )
    bias = gather_cores(pieces, gather_sides(pieces))

    residue_live = residue_mask.astype(f32)
    key_bias = jnp.broadcast_to(((residue_live - 1.0) * 1000000000.0)[:, None], (512, 128))
    cols_live = lax.dynamic_slice_in_dim(residue_live, head_index * 64, 64)
    rows_live = lax.dynamic_slice_in_dim(residue_live, row_index * 16, 16)
    row_live = alignment_row_mask.astype(f32)
    live = (row_live[:, None] * cols_live[None, :]).reshape(128, 1)
    mask_tile = jnp.zeros((8, 128), f32).at[0, 0:2].set(row_live)
    spots = jnp.asarray(SPOTS.reshape(-1))
    once = jnp.asarray(ONCE.reshape(-1))
    logits, values, gate = call(
        logits_kernel,
        vmem(7),
        vmem(3),
        [struct(2, 512, 512), struct(2, 2, 256, 512, dtype=bf16), struct(128, 256)],
        flops=3 * 2 * 1024 * 256 * 1024,
        touched=6 * MIB,
    )(
        everyone,
        sequence_matrix,
        attention_scale_vector[None],
        asking_factor_matrix,
        lookup_factor_matrix,
        content_factor_matrix,
        sigmoid_factor_matrix,
    )
    msa_out, left, right = call(
        attend_kernel,
        smem(1) + vmem(19),
        vmem(3),
        [struct(2, 64, 256), struct(4, 8, 128), struct(Z, 40, 128)],
        scratch=[pltpu.VMEM((32, 64, 128), f32), pltpu.VMEM((128, 128), f32)],
        flops=3 * 2 * 1024 * 512 * 256,
        touched=6 * MIB,
    )(
        spots,
        *bias,
        logits,
        key_bias,
        values,
        gate,
        sequence_matrix,
        final_factor_matrix,
        tensor_scale_vector[None],
        jnp.tile(first_factor_matrix, (1, 4)),
        second_factor_matrix.T,
        live,
        mask_tile,
    )
    planes = lax.all_to_all(
        right,
        "row",
        0,
        0,
        tiled=True,
        axis_index_groups=[[4 * z + a for z in range(Z)] for a in range(A)],
    )
    left = lax.ppermute(left, both, [(d, s) for s, d in moves(ONCE)])
    (spread,) = call(
        spread_kernel,
        vmem(1),
        hbm(1),
        [struct(A, H, 8, 128)],
        scratch=[pltpu.SemaphoreType.DMA((H,))],
    )(left)
    left = lax.all_to_all(
        spread.reshape(A * H, 8, 128),
        both,
        0,
        0,
        tiled=True,
        axis_index_groups=[[32 * z + k for k in range(32)] for z in range(Z)],
    )
    right = gather_cores([planes], after(gather_sides(after([planes], spread)), left))
    (pair_out,) = call(
        outer_kernel,
        smem(2) + vmem(8),
        vmem(1),
        [struct(16, 64, 128)],
        scratch=[
            pltpu.VMEM((1280, 128), f32),
            pltpu.VMEM((256, 128), f32),
            pltpu.VMEM((512, 256), bf16),
            pltpu.VMEM((256, 2048), bf16),
            pltpu.VMEM((512, 2048), f32),
        ],
        flops=3 * 2 * 1024 * 1024 * 256,
        touched=4 * MIB,
    )(
        once,
        rows_live,
        *right,
        left,
        outer_weight,
        pair_representation,
        cols_live[:, None],
    )
    return msa_out, pair_out


def solution(mesh):
    cells = P("row", "head", None)
    return jax.shard_map(
        body,
        mesh=mesh,
        in_specs=(cells, cells, P("row")) + (P(),) * 13,
        out_specs=(cells, cells),
        check_vma=False,
    )
```

```python
import itertools
import math

import jax
import jax.numpy as jnp
import numpy as np
from jax import lax
from jax.experimental import pallas as pl
from jax.experimental.pallas import tpu as pltpu
from jax.sharding import PartitionSpec as P

exact = lax.Precision.HIGHEST
f32 = jnp.float32
bf16 = jnp.bfloat16
MIB = 1024 * 1024

Z, A, H = 8, 4, 8
def ring(d, n):
    return min(d % n, -d % n)


def spread_tables():
    once = np.zeros((H, H), np.int32)
    twice = np.zeros((H, 2, H), np.int32)
    for c in range(H):
        hops = [
            [ring(h // 2 - c // 2, 4) + 2 * ((h ^ c) & 1) + ring(b - c, Z) for b in range(Z)]
            for h in range(H)
        ]
        flat = [hops[h][c] for h in range(H)]
        columns = sorted(range(H), key=lambda h: (-flat[h], (h // 2 - c // 2) % 4))
        planes = sorted(range(Z), key=lambda b: (ring(b - c, Z), (b - c) % Z))
        for h, b in zip(columns, planes):
            once[c][h] = b

        def fit(group, half):
            return min(
                (
                    (max(hops[h][b] for h, b in zip(group, p)), sum(hops[h][b] for h, b in zip(group, p)), p)
                    for p in itertools.permutations(range(4 * half, 4 * half + 4))
                )
            )

        best = None
        for low in itertools.combinations(range(H), 4):
            high = tuple(h for h in range(H) if h not in low)
            first = fit(low, 0), fit(high, 1)
            second = fit(low, 1), fit(high, 0)
            cost = (
                max(first[0][0], first[1][0]) + max(second[0][0], second[1][0]),
                sum(f[1] for f in first + second),
            )
            if best is None or cost < best[0]:
                best = cost, low, high, first, second
        _, low, high, first, second = best
        if max(f[0] for f in first) < max(f[0] for f in second):
            first, second = second, first
        for k, fits in enumerate((first, second)):
            for group, found in zip((low, high), fits):
                for h, b in zip(group, found[2]):
                    twice[c][k][h] = b
    return once, twice


ONCE, TWICE = spread_tables()


def moves(table):
    return [
        ((4 * b + a) * H + h, (4 * int(table[b][h]) + a) * H + b)
        for b in range(Z)
        for a in range(A)
        for h in range(H)
    ]


def spots():
    out = np.zeros((H, 2, H), np.int32)
    for c in range(H):
        for k in range(2):
            for h in range(H):
                plane = int(TWICE[c][k][h])
                out[c][plane // 4][h] = 4 * k + plane % 4
    return out


SPOTS = spots()


def from_neighbour(v, bit):
    return lax.ppermute(v, "row", [(r, r ^ bit) for r in range(Z * A)])


def after(values, *others):
    return list(lax.optimization_barrier((*values, *others)))[: len(values)]


def gather_halves(first, second):
    own = jnp.concatenate([first, second], axis=0)
    near = jnp.concatenate([own, from_neighbour(own, 8)], axis=0)
    return [near, from_neighbour(near, 4)]


def gather_sides(pieces):
    return [from_neighbour(p, 2) for p in pieces]


def gather_cores(pieces, sides):
    return (
        pieces
        + [from_neighbour(p, 1) for p in pieces]
        + sides
        + [from_neighbour(p, 1) for p in sides]
    )


def side_of(row, source_side):
    return jnp.bitwise_xor(jnp.bitwise_and(row, 3), source_side) * 8


def half_position(row, spot, source_side):
    plane = jnp.bitwise_xor(jnp.bitwise_and(jnp.right_shift(row, 2), 3), jnp.bitwise_and(spot, 3))
    return (
        side_of(row, source_side)
        + jnp.bitwise_and(plane, 1) * 4
        + jnp.bitwise_and(plane, 2)
        + jnp.right_shift(spot, 2)
    )


def split(v):
    high = v.astype(bf16)
    return high, (v - high.astype(f32)).astype(bf16)


def dot(a, b, dims=((1,), (0,))):
    return lax.dot_general(a, b, (dims, ((), ())), preferred_element_type=f32)


def dot_exact(a, b, dims=((1,), (0,))):
    return lax.dot_general(a, b, (dims, ((), ())), precision=exact, preferred_element_type=f32)


def three(a, b, dims=((1,), (0,))):
    return dot(a[0], b[0], dims) + (dot(a[0], b[1], dims) + dot(a[1], b[0], dims))


def dot_three(a, b, dims=((1,), (0,))):
    return three(split(a), split(b), dims)


def norm_rows(v, gain):
    center = v - jnp.mean(v, axis=-1, keepdims=True)
    spread = jnp.mean(center * center, axis=-1, keepdims=True)
    return center * lax.rsqrt(spread + 1e-05) * gain


def start_all(copies):
    for copy in copies:
        copy.start()
    return copies


def wait_all(copies):
    for copy in copies:
        copy.wait()


def bias_kernel(
    pair_hbm,
    gain_hbm,
    weight_hbm,
    own_hbm,
    out_ref,
    copies_hbm,
    pair_ref,
    gain_ref,
    weight_ref,
    own_ref,
    sems,
):
    own_load = start_all([pltpu.make_async_copy(own_hbm, own_ref, sems.at[11])])
    loads = start_all(
        [
            pltpu.make_async_copy(gain_hbm, gain_ref, sems.at[8]),
            pltpu.make_async_copy(weight_hbm, weight_ref, sems.at[9]),
            pltpu.make_async_copy(pair_hbm, pair_ref, sems.at[10]),
        ]
    )
    wait_all(own_load)
    copies = start_all(
        [pltpu.make_async_copy(own_ref, copies_hbm.at[k], sems.at[k]) for k in range(H)]
    )
    wait_all(loads)
    rows = pair_ref[...].reshape(1024, 128)
    normed = norm_rows(rows, gain_ref[...])
    pick = lax.broadcasted_iota(jnp.int32, (8, 128), 0) == (
        lax.broadcasted_iota(jnp.int32, (8, 128), 1) // 16
    )
    wide = dot_exact(weight_ref[...], jnp.where(pick, 1.0, 0.0), ((0,), (0,)))
    result = dot_exact(normed, wide)
    lane = lax.broadcasted_iota(jnp.int32, (64, 128), 1) % 16
    total = jnp.zeros((64, 128), f32)
    for i in range(16):
        total = jnp.where(lane == i, result[64 * i : 64 * i + 64], total)
    out_ref[0] = total
    wait_all(copies)


def spread_kernel(left_ref, out_ref, sems):
    wait_all(
        start_all(
            [pltpu.make_async_copy(left_ref, out_ref.at[:, k], sems.at[k]) for k in range(H)]
        )
    )


def logits_kernel(
    all_ref, own_ref, gain_ref, wq_ref, wk_ref, wv_ref, wg_ref, logit_ref, value_ref, gate_ref
):
    gain = gain_ref[...]
    own = split(norm_rows(own_ref[...].reshape(128, 256), gain))
    query = three(own, split(wq_ref[...])) * (1.0 / math.sqrt(32))
    gate_ref[...] = jax.nn.sigmoid(three(own, split(wg_ref[...])))
    head_of_lane = lax.broadcasted_iota(jnp.int32, (128, 256), 1) // 32
    head_of_row = lax.broadcasted_iota(jnp.int32, (128, 256), 0) // 16
    keep = head_of_lane == head_of_row
    key_factor = split(wk_ref[...])
    value_factor = split(jnp.transpose(wv_ref[...]))
    for s in range(2):
        rows = split(
            norm_rows(jnp.concatenate([all_ref[b, s] for b in range(8)], axis=0), gain)
        )
        keys = split(three(rows, key_factor))
        value_ref[0, s], value_ref[1, s] = split(three(value_factor, rows, ((1,), (1,))))
        wide = []
        for a in range(4):
            part = query[64 * s + 16 * a : 64 * s + 16 * a + 16]
            wide.append(jnp.where(keep, jnp.concatenate([part] * 8, axis=0), 0.0))
        logit_ref[s] = three(keys, split(jnp.concatenate(wide, axis=0)), ((1,), (1,)))


def attend_kernel(
    spot_ref,
    *refs,
):
    attend(spot_ref, refs[:8], *refs[8:])


def attend(
    spot_ref,
    piece_refs,
    logit_ref,
    key_ref,
    value_ref,
    gate_ref,
    own_ref,
    wf_ref,
    gain_ref,
    first_ref,
    second_ref,
    live_ref,
    mask_ref,
    msa_ref,
    left_ref,
    right_ref,
    bias_ref,
    y_ref,
):
    for k, piece_ref in enumerate(piece_refs):
        bias_ref[4 * k : 4 * k + 4] = piece_ref[...]
    row = lax.axis_index("row")
    spots_at = (lax.axis_index("head") * 2 + jnp.right_shift(row, 4)) * H
    lane = lax.broadcasted_iota(jnp.int32, (32, 128), 1) // 16
    folded = [jnp.zeros((32, 128), f32) for _ in range(8)]
    for s in range(2):
        for pair in range(2):
            halves = []
            for a in (2 * pair, 2 * pair + 1):
                columns = pl.ds(128 * a, 128)
                tiles = []
                for b in range(8):
                    rows = pl.ds(64 * b, 64)
                    spot = half_position(row, spot_ref[spots_at + b], a)
                    tiles.append((logit_ref[s, rows, columns] + bias_ref[spot]) + key_ref[rows, :])
                logits = jnp.concatenate(tiles, axis=0)
                exponent = jnp.exp(logits - jnp.max(logits, axis=0, keepdims=True))
                weights = exponent * (1.0 / jnp.sum(exponent, axis=0, keepdims=True))
                halves.append(split(weights))
            part = three(
                (value_ref[0, s], value_ref[1, s]),
                [jnp.concatenate([halves[0][k], halves[1][k]], axis=1) for k in range(2)],
            )
            for e in range(2):
                a = 2 * pair + e
                for h in range(8):
                    moved = pltpu.roll(
                        part[32 * h : 32 * h + 32, 128 * e : 128 * e + 128],
                        (64 * s + 16 * a - 16 * h) % 128,
                        1,
                    )
                    folded[h] = jnp.where(lane == 4 * s + a, moved, folded[h])
    attended = jnp.transpose(jnp.concatenate(folded, axis=0)) * gate_ref[...]
    updated = own_ref[...].reshape(128, 256) + dot_three(attended, wf_ref[...])
    msa_ref[...] = updated.reshape(2, 64, 256)
    y = norm_rows(updated, gain_ref[...]) * live_ref[...]
    y = split(y)
    right = three(split(second_ref[...]), y, ((1,), (1,)))
    for k in range(Z):
        right_ref[k, 0:32, :] = right
        right_ref[k, 32:40, :] = mask_ref[...]
    y_ref[...] = three(y, split(first_ref[...]))
    lane = lax.broadcasted_iota(jnp.int32, (32, 128), 1) // 32
    left = jnp.zeros((32, 128), f32)
    for k in range(4):
        left = jnp.where(lane == k, y_ref[pl.ds(k, 32, stride=4), :], left)
    for s in range(2):
        for a in range(4):
            left_ref[a, 4 * s : 4 * s + 4, :] = left[16 * s + 4 * a : 16 * s + 4 * a + 4]


def outer_kernel(
    once_ref,
    rows_live_ref,
    *refs,
):
    outer_product(once_ref, rows_live_ref, refs[:4], *refs[4:])


def outer_product(
    once_ref,
    rows_live_ref,
    piece_refs,
    left_in_ref,
    weight_ref,
    pair_ref,
    cols_live_ref,
    out_hbm,
    right_in_ref,
    sorted_ref,
    left_ref,
    right_ref,
    outer_ref,
    out_ref,
    sems,
):
    for q, piece_ref in enumerate(piece_refs):
        for k in range(Z):
            start = 40 * (Z * q + k)
            right_in_ref[start : start + 40, :] = piece_ref[k]
    row = lax.axis_index("row")
    for p in range(32):
        source = side_of(row, p // H) + once_ref[jnp.right_shift(row, 2) * H + p % H]
        spot = pl.multiple_of(source * 8, 8)
        sorted_ref[pl.ds(spot, 8), :] = left_in_ref[p]
    count = jnp.zeros((8, 128), f32)
    for k in range(32):
        count = count + right_in_ref[40 * k + 32 : 40 * k + 40, :]
    count = jnp.sum(count)
    left_rows = []
    for s in range(2):
        left_rows.append(
            jnp.concatenate(
                [sorted_ref[pl.ds(4 * s + q, 32, stride=8), :] for q in range(4)], axis=1
            )
        )
    left = jnp.concatenate(left_rows, axis=0)
    high = left.astype(bf16).astype(f32)
    halves = jnp.transpose(jnp.concatenate([high, left - high], axis=0))
    lane = lax.broadcasted_iota(jnp.int32, (512, 128), 1) < 64
    left_ref[:, 0:128] = halves.astype(bf16)
    left_ref[:, 128:256] = jnp.where(lane, halves, 0.0).astype(bf16)
    lane = lax.broadcasted_iota(jnp.int32, (32, 128), 1) < 64
    for d in range(16):
        even = right_in_ref[pl.ds(2 * d, 32, stride=40), :]
        odd = right_in_ref[pl.ds(2 * d + 1, 32, stride=40), :]
        both = jnp.concatenate(
            [
                jnp.where(lane, even, pltpu.roll(odd, 64, 1)),
                jnp.where(lane, pltpu.roll(even, 64, 1), odd),
            ],
            axis=0,
        )
        high, low = split(both)
        columns = pl.ds(128 * d, 128)
        right_ref[0:64, columns] = high
        right_ref[64:128, columns] = high
        right_ref[128:192, columns] = low
        right_ref[192:256, columns] = jnp.zeros((64, 128), bf16)
    columns = [
        jnp.concatenate(
            [weight_ref[pl.ds(2 * d + e, 32, stride=32), :] for d in range(16)], axis=0
        )
        for e in range(2)
    ]
    weight = split(jnp.transpose(jnp.concatenate(columns, axis=1)))
    lane = lax.broadcasted_iota(jnp.int32, (128, 128), 1) < 64
    for n in range(8):
        columns = pl.ds(256 * n, 256)
        outer_ref[:, columns] = dot(left_ref[...], right_ref[:, columns])
    stores = []
    for q in range(8):
        stacked = jnp.concatenate(
            [
                jnp.concatenate(
                    [
                        outer_ref[64 * q + 32 * e : 64 * q + 32 * e + 32, 128 * d : 128 * d + 128]
                        for d in range(16)
                    ],
                    axis=0,
                )
                for e in range(2)
            ],
            axis=1,
        )
        y = three(weight, split(stacked))
        top, bottom = y[0:128], y[128:256]
        total = jnp.where(
            lane,
            top[:, 0:128] + pltpu.roll(bottom[:, 0:128], 64, 1),
            pltpu.roll(top[:, 128:256], 64, 1) + bottom[:, 128:256],
        )
        total = jnp.transpose(total)
        for e in range(2):
            i = 2 * q + e
            norm = count * rows_live_ref[i] * cols_live_ref[...] + 0.001
            out_ref[i] = pair_ref[i] + total[64 * e : 64 * e + 64] / norm
        stores += start_all(
            [
                pltpu.make_async_copy(
                    out_ref.at[2 * q : 2 * q + 2], out_hbm.at[2 * q : 2 * q + 2], sems.at[q]
                )
            ]
        )
    wait_all(stores)


def vmem(count):
    return [pl.BlockSpec(memory_space=pltpu.VMEM)] * count


def smem(count):
    return [pl.BlockSpec(memory_space=pltpu.SMEM)] * count


def hbm(count):
    return [pl.BlockSpec(memory_space=pltpu.HBM)] * count


def struct(*shape, dtype=f32):
    return jax.ShapeDtypeStruct(shape, dtype)


def call(kernel, inputs, outputs, shapes, scratch=(), limit=32, flops=0, touched=0):
    return pl.pallas_call(
        kernel,
        in_specs=inputs,
        out_specs=outputs,
        out_shape=shapes,
        scratch_shapes=list(scratch),
        compiler_params=pltpu.CompilerParams(vmem_limit_bytes=limit * MIB),
        cost_estimate=pl.CostEstimate(flops=flops, bytes_accessed=touched, transcendentals=0),
    )


def body(
    sequence_matrix,
    pair_representation,
    alignment_row_mask,
    residue_mask,
    attention_scale_vector,
    asking_factor_matrix,
    lookup_factor_matrix,
    content_factor_matrix,
    sigmoid_factor_matrix,
    final_factor_matrix,
    pair_norm_gain,
    bias_weight,
    tensor_scale_vector,
    first_factor_matrix,
    second_factor_matrix,
    outer_weight,
):
    head_index = lax.axis_index("head")
    row_index = lax.axis_index("row")
    both = ("row", "head")
    block, copies = call(
        bias_kernel,
        hbm(4),
        vmem(1) + hbm(1),
        [struct(1, 64, 128), struct(H, 2, 64, 256)],
        scratch=[
            pltpu.VMEM((16, 64, 128), f32),
            pltpu.VMEM((1, 128), f32),
            pltpu.VMEM((8, 128), f32),
            pltpu.VMEM((2, 64, 256), f32),
            pltpu.SemaphoreType.DMA((H + 4,)),
        ],
        limit=60,
        flops=2 * 1024 * 128 * 128 * 6,
        touched=600000,
    )(pair_representation, pair_norm_gain[None], bias_weight.T, sequence_matrix)
    everyone = lax.all_to_all(copies, "head", 0, 0, tiled=True)
    pieces = gather_halves(
        lax.ppermute(block, both, moves(TWICE[:, 0])), lax.ppermute(block, both, moves(TWICE[:, 1]))
    )
    bias = gather_cores(pieces, gather_sides(pieces))

    residue_live = residue_mask.astype(f32)
    key_bias = jnp.broadcast_to(((residue_live - 1.0) * 1000000000.0)[:, None], (512, 128))
    cols_live = lax.dynamic_slice_in_dim(residue_live, head_index * 64, 64)
    rows_live = lax.dynamic_slice_in_dim(residue_live, row_index * 16, 16)
    row_live = alignment_row_mask.astype(f32)
    live = (row_live[:, None] * cols_live[None, :]).reshape(128, 1)
    mask_tile = jnp.zeros((8, 128), f32).at[0, 0:2].set(row_live)
    spots = jnp.asarray(SPOTS.reshape(-1))
    once = jnp.asarray(ONCE.reshape(-1))
    logits, values, gate = call(
        logits_kernel,
        vmem(7),
        vmem(3),
        [struct(2, 512, 512), struct(2, 2, 256, 512, dtype=bf16), struct(128, 256)],
        flops=3 * 2 * 1024 * 256 * 1024,
        touched=6 * MIB,
    )(
        everyone,
        sequence_matrix,
        attention_scale_vector[None],
        asking_factor_matrix,
        lookup_factor_matrix,
        content_factor_matrix,
        sigmoid_factor_matrix,
    )
    msa_out, left, right = call(
        attend_kernel,
        smem(1) + vmem(19),
        vmem(3),
        [struct(2, 64, 256), struct(4, 8, 128), struct(Z, 40, 128)],
        scratch=[pltpu.VMEM((32, 64, 128), f32), pltpu.VMEM((128, 128), f32)],
        flops=3 * 2 * 1024 * 512 * 256,
        touched=6 * MIB,
    )(
        spots,
        *bias,
        logits,
        key_bias,
        values,
        gate,
        sequence_matrix,
        final_factor_matrix,
        tensor_scale_vector[None],
        jnp.tile(first_factor_matrix, (1, 4)),
        second_factor_matrix.T,
        live,
        mask_tile,
    )
    planes = lax.all_to_all(
        right,
        "row",
        0,
        0,
        tiled=True,
        axis_index_groups=[[4 * z + a for z in range(Z)] for a in range(A)],
    )
    left = lax.ppermute(left, both, [(d, s) for s, d in moves(ONCE)])
    (spread,) = call(
        spread_kernel,
        vmem(1),
        hbm(1),
        [struct(A, H, 8, 128)],
        scratch=[pltpu.SemaphoreType.DMA((H,))],
    )(left)
    left = lax.all_to_all(
        spread.reshape(A * H, 8, 128),
        both,
        0,
        0,
        tiled=True,
        axis_index_groups=[[32 * z + k for k in range(32)] for z in range(Z)],
    )
    right = gather_cores([planes], after(gather_sides(after([planes], spread)), left))
    (pair_out,) = call(
        outer_kernel,
        smem(2) + vmem(8),
        hbm(1),
        [struct(16, 64, 128)],
        scratch=[
            pltpu.VMEM((1280, 128), f32),
            pltpu.VMEM((256, 128), f32),
            pltpu.VMEM((512, 256), bf16),
            pltpu.VMEM((256, 2048), bf16),
            pltpu.VMEM((512, 2048), f32),
            pltpu.VMEM((16, 64, 128), f32),
            pltpu.SemaphoreType.DMA((8,)),
        ],
        flops=3 * 2 * 1024 * 1024 * 256,
        touched=4 * MIB,
    )(
        once,
        rows_live,
        *right,
        left,
        outer_weight,
        pair_representation,
        cols_live[:, None],
    )
    return msa_out, pair_out


def solution(mesh):
    cells = P("row", "head", None)
    return jax.shard_map(
        body,
        mesh=mesh,
        in_specs=(cells, cells, P("row")) + (P(),) * 13,
        out_specs=(cells, cells),
        check_vma=False,
    )
```
